256 devices in a mesh: edges: 256 (over y, z, x, core).
Axes of the slice: x: 4, y: 4, z: 8, core: 2. Of those that a mesh axis runs over, the one named last changes fastest.
Arguments:
- messages: float32 [98304, 512], P('edges'), may hold values from -6 to 6
- rev_slot: int32 [98304], P('edges'), may hold values from 0 to 95, as said below
- tri_basis: float32 [16, 393216], P(None, 'edges'), may hold values from -6 to 6
- tri_source: int32 [393216], P('edges'), may hold values from 0 to 575
- tri_target: int32 [393216], P('edges'), may hold values from 0 to 127
- tile_block: int32 [3072], P('edges'), may hold values from 0 to 2
- tile_count: int32 [256], P('edges'), may hold values from 6 to 12, as said below
- w_basis: float32 [16, 512], replicated, may hold values from -1.5 to 1.5
- w_rev: float32 [512, 512], replicated, may hold values from -0.25 to 0.25
- w_layers: float32 [2, 512, 512], replicated, may hold values from -0.25 to 0.25
- cotangent: float32 [98304, 512], P('edges'), may hold values from -6 to 6
Outputs:
- out_messages: float32 [98304, 512], P('edges')
- grad_messages: float32 [98304, 512], P('edges')
- grad_layers: float32 [2, 262144], P(None, 'edges')
- grad_rev: float32 [262144], P('edges')
- grad_basis: float32 [16, 512], replicated
The draws below stay inside these ranges and needn't reach their ends.
Inputs may be any that keep to these rules, and one draw needn't show every extreme that they name: rev_slot pairs every edge with a reverse edge as in the reference program, and the pairing is an involution: the reverse of an edge's reverse is the edge itself. Tiles j >= tile_count[d] of device d are ignored whatever they hold; some device has 12 live tiles.
All inputs are finite; a program needn't handle non-finite values.
Results may differ from the reference program's by a relative error of at most 0.0003.
Values sent between devices are 32-bit elements; how exact they have to be, the bound alone decides.
No kernel may reach another device: no remote copies, remote signals or barrier semaphores. Data moves between devices by JAX's collectives and lax.ppermute only.
A program may use at most 64 MiB of HBM per device.

```python
import jax
import jax.numpy as jnp
import numpy as np
from jax import lax

D = 512
NB = 16
LAYERS = 2
E_DEV = 384
TILE_CAP = 12
HALO = 96
GROUP = 96
EDGES = 98304
TILES = 3072
TRIPS = 393216
N_EDGES = 256


def draw_tile_count(key, part):
    counts = jax.random.randint(jax.random.fold_in(key, 11), (N_EDGES,), TILE_CAP // 2, TILE_CAP + 1)
    busiest = jax.random.randint(jax.random.fold_in(key, 12), (), 0, N_EDGES)
    return jnp.where(jnp.arange(N_EDGES) == busiest, TILE_CAP, counts).astype(jnp.int32)


def draw_rev_slot(key, part):
    levels = N_EDGES.bit_length() - 1
    bit_table = jnp.asarray(np.array([0, levels // 3, 2 * levels // 3, levels - 1], np.int32))
    base_key = jax.random.fold_in(key, 21)

    def one_group(device, group_id):
        bit_pos = bit_table[group_id]
        upper = jnp.bitwise_and(jnp.right_shift(device, bit_pos), 1)
        lower_dev = device - upper * jnp.left_shift(jnp.int32(1), bit_pos)
        order = jax.random.permutation(jax.random.fold_in(base_key, lower_dev * 4 + group_id), GROUP)
        inverse = jnp.argsort(order)
        return jnp.where(upper == 1, inverse, order)

    def one_device(device):
        return jax.vmap(lambda group_id: one_group(device, group_id))(jnp.arange(4, dtype=jnp.int32))
    table = jax.vmap(one_device)(jnp.arange(N_EDGES, dtype=jnp.int32))
    return table.reshape(N_EDGES * E_DEV).astype(jnp.int32)


def touch_ends(drawn, stream_key, least, top_value):
    extent = drawn.shape
    place = [jax.random.randint(jax.random.fold_in(stream_key, axis), (), 0, extent[axis]) for axis in range(len(extent))]
    drawn = drawn.at[tuple(place)].set(least)
    longest = extent.index(max(extent))
    place[longest] = (place[longest] + 1) % extent[longest]
    return drawn.at[tuple(place)].set(top_value)


def block_levels(own_key, shape, shards, low, top_value):
    level, own = 1.0, jax.random.fold_in(own_key, 6)
    for position, parts in shards:
        draws = jnp.exp(jax.random.uniform(jax.random.fold_in(own, position), (parts,), jnp.float32, low / len(shards), top_value / len(shards)))
        level = level * jnp.repeat(draws, shape[position] // parts).reshape([-1 if axis == position else 1 for axis in range(len(shape))])
    return level


def centred(rng, extent, spread, bound, split=(), held_as=jnp.bfloat16):
    level = block_levels(rng, extent, split, -0.22, 0.18) if split else 1.0
    values = jax.random.normal(rng, extent, jnp.float32) * spread * level
    return jnp.minimum(jnp.maximum(values, -bound), bound).astype(held_as)


def setup_inputs(seed: int = 0) -> dict:
    key_list = jax.random.split(jax.random.key(seed), 12)
    return {
        "messages": centred(key_list[0], (EDGES, D), 1.0, 6.0, ((0, 256),), jnp.float32),
        "rev_slot": draw_rev_slot(jax.random.fold_in(key_list[11], 71), 0),
        "tri_basis": centred(key_list[2], (NB, TRIPS), 1.0, 6.0, ((1, 256),), jnp.float32),
        "tri_source": touch_ends(jax.random.randint(key_list[3], (TRIPS,), 0, E_DEV + 2 * HALO), jax.random.fold_in(key_list[3], 1), 0, (E_DEV + 2 * HALO) - 1).astype(jnp.int32),
        "tri_target": touch_ends(jax.random.randint(key_list[4], (TRIPS,), 0, 128), jax.random.fold_in(key_list[4], 1), 0, 127).astype(jnp.int32),
        "tile_block": touch_ends(jax.random.randint(key_list[5], (TILES,), 0, E_DEV // 128), jax.random.fold_in(key_list[5], 1), 0, (E_DEV // 128) - 1).astype(jnp.int32),
        "tile_count": draw_tile_count(jax.random.fold_in(key_list[11], 71), 0),
        "w_basis": centred(key_list[7], (NB, D), NB ** -0.5, 1.5, (), jnp.float32),
        "w_rev": centred(key_list[8], (D, D), D ** -0.5, 0.25, (), jnp.float32),
        "w_layers": centred(key_list[9], (LAYERS, D, D), D ** -0.5, 0.25, (), jnp.float32),
        "cotangent": centred(key_list[10], (EDGES, D), 1.0, 6.0, ((0, 256),), jnp.float32),
    }


def full_dot(left, right):
    return jnp.dot(left, right, precision=lax.Precision.HIGHEST, preferred_element_type=jnp.float32)


def lead_dot(left, right):
    return lax.dot_general(left, right, (((0,), (0,)), ((), ())), precision=lax.Precision.HIGHEST, preferred_element_type=jnp.float32)


def trail_dot(left, right):
    return lax.dot_general(left, right, (((1,), (1,)), ((), ())), precision=lax.Precision.HIGHEST, preferred_element_type=jnp.float32)


def silu_slope(values):
    sigma = jax.nn.sigmoid(values)
    return sigma * (1.0 + values * (1.0 - sigma))


def partner_index(rev_slot):
    levels = N_EDGES.bit_length() - 1
    bit_table = jnp.asarray(np.array([0, levels // 3, 2 * levels // 3, levels - 1], np.int32))
    flat = jnp.arange(N_EDGES * E_DEV, dtype=jnp.int32)
    device = flat // E_DEV
    group_id = (flat % E_DEV) // GROUP
    partner = jnp.bitwise_xor(device, jnp.left_shift(jnp.int32(1), bit_table[group_id]))
    return (partner * E_DEV + group_id * GROUP + rev_slot).astype(jnp.int32)


def reference(messages, rev_slot, tri_basis, tri_source, tri_target, tile_block, tile_count, w_basis, w_rev, w_layers, cotangent):
    slots = TILE_CAP * 128
    scale = float(EDGES) ** -0.5
    stacked = messages.reshape(N_EDGES, E_DEV, D)
    partner = partner_index(rev_slot)
    rev_msg = jnp.take(messages, partner, axis=0)
    rev_proj = full_dot(rev_msg, w_rev)
    gate_vals = jax.nn.silu(rev_proj)

    def device_tiles(device):
        before = lax.dynamic_index_in_dim(stacked, (device + N_EDGES - 1) % N_EDGES, 0, keepdims=False)
        own = lax.dynamic_index_in_dim(stacked, device, 0, keepdims=False)
        after = lax.dynamic_index_in_dim(stacked, (device + 1) % N_EDGES, 0, keepdims=False)
        window = jnp.concatenate([before[E_DEV - HALO:], own, after[:HALO]], axis=0)
        source = lax.dynamic_slice_in_dim(tri_source, device * slots, slots)
        target = lax.dynamic_slice_in_dim(tri_target, device * slots, slots)
        blocks = lax.dynamic_slice_in_dim(tile_block, device * TILE_CAP, TILE_CAP)
        coeffs = lax.dynamic_slice_in_dim(tri_basis, device * slots, slots, 1)
        live_tiles = (jnp.arange(TILE_CAP, dtype=jnp.int32) < tile_count[device]).astype(jnp.float32)
        live = jnp.repeat(live_tiles, 128)
        edge_row = (jnp.repeat(blocks, 128) * 128 + target).astype(jnp.int32)
        gathered = jnp.take(window, source, axis=0)
        tri_weight = lead_dot(coeffs, w_basis)
        return source, edge_row, live, gathered, tri_weight, coeffs

    def forward_agg(device):
        source, edge_row, live, gathered, tri_weight, coeffs = device_tiles(device)
        terms = gathered * tri_weight * live[:, None]
        return jax.ops.segment_sum(terms, edge_row, num_segments=E_DEV)

    devices = jnp.arange(N_EDGES, dtype=jnp.int32)
    agg = lax.map(forward_agg, devices).reshape(N_EDGES * E_DEV, D)
    hidden = messages + agg + messages * gate_vals
    states = [hidden]
    pre_list = []
    for layer in range(LAYERS):
        pre_act = full_dot(hidden, w_layers[layer])
        pre_list.append(pre_act)
        hidden = hidden + jax.nn.silu(pre_act)
        states.append(hidden)
    out_messages = hidden

    grad = cotangent
    layer_grads = [None] * LAYERS
    for layer in range(LAYERS - 1, -1, -1):
        grad_pre = grad * silu_slope(pre_list[layer])
        layer_grads[layer] = (lead_dot(states[layer], grad_pre) * scale).reshape(D * D)
        grad = grad + trail_dot(grad_pre, w_layers[layer])
    grad_agg = grad
    grad_msg = grad * (1.0 + gate_vals)
    grad_rev_proj = grad * messages * silu_slope(rev_proj)
    grad_rev = (lead_dot(rev_msg, grad_rev_proj) * scale).reshape(D * D)
    grad_rows = trail_dot(grad_rev_proj, w_rev)
    grad_msg = grad_msg + jnp.take(grad_rows, partner, axis=0)
    grad_stack = grad_agg.reshape(N_EDGES, E_DEV, D)

    def backward_tiles(device):
        source, edge_row, live, gathered, tri_weight, coeffs = device_tiles(device)
        own_grad = lax.dynamic_index_in_dim(grad_stack, device, 0, keepdims=False)
        grad_prod = jnp.take(own_grad, edge_row, axis=0) * live[:, None]
        window_grad = jax.ops.segment_sum(grad_prod * tri_weight, source, num_segments=E_DEV + 2 * HALO)
        basis_part = full_dot(coeffs, grad_prod * gathered)
        return window_grad, basis_part

    window_grads, basis_parts = lax.map(backward_tiles, devices)
    result = grad_msg.reshape(N_EDGES, E_DEV, D) + window_grads[:, HALO:HALO + E_DEV]
    result = result.at[:, E_DEV - HALO:].add(jnp.roll(window_grads[:, :HALO], -1, axis=0))
    result = result.at[:, :HALO].add(jnp.roll(window_grads[:, HALO + E_DEV:], 1, axis=0))
    grad_basis = jnp.sum(basis_parts, axis=0) * scale
    return (out_messages, result.reshape(N_EDGES * E_DEV, D), jnp.stack(layer_grads), grad_rev, grad_basis)
```

```python
import jax
import jax.numpy as jnp
from jax import lax
from jax.experimental import pallas as pl
from jax.experimental.pallas import tpu as pltpu
from jax.sharding import PartitionSpec as P


F32, BF16, I32 = jnp.float32, jnp.bfloat16, jnp.int32
D, E, HALO, SLOTS, TILES = 512, 384, 96, 1536, 12
WIN = E + 2 * HALO
CHUNK = 512


def split(value):
    high = value.astype(BF16)
    return high, (value - high.astype(F32)).astype(BF16)


def nn(a, b):
    return lax.dot_general(a, b, (((1,), (0,)), ((), ())), preferred_element_type=F32)


def nt(a, b):
    return lax.dot_general(a, b, (((1,), (1,)), ((), ())), preferred_element_type=F32)


def tn(a, b):
    return lax.dot_general(a, b, (((0,), (0,)), ((), ())), preferred_element_type=F32)


def dot3(op, a, b):
    return op(a[0], b[0]) + (op(a[1], b[0]) + op(a[0], b[1]))


def onehot(test):
    return jnp.where(test, 1.0, 0.0).astype(BF16)


def flip2(bits):
    return ((bits & 1) << 1) + ((bits >> 1) & 1)


def flip3(bits):
    return ((bits & 1) << 2) + (bits & 2) + ((bits >> 2) & 1)


def prepare(
    me, count, blocks, src, tgt, rev, coeffs, wb, m, wr, wl,
    gath, tw, oh2, ot, t2, tt, r, rt, pick, wr_hi, wr_lo, wl_hi, wl_lo,
    o2, m2, c3, w3,
):
    lane = lax.broadcasted_iota(I32, (128, 128), 1).astype(F32)
    sub = lax.broadcasted_iota(I32, (128, 128), 0)
    n_live = count[0]

    def tile(j, carry):
        at = pl.ds(pl.multiple_of(j * 128, 128), 128)
        w = src[:, at]
        u = jnp.where(w >= HALO, w - HALO, w + (E + HALO))
        live = j < n_live
        t = jnp.where(live, tgt[:, at] + blocks[j] * 128, -1)
        ub = jnp.broadcast_to(u, (128, 128))
        tb = jnp.broadcast_to(t, (128, 128))
        for k in range(5):
            rows = 128 if k < 4 else 64
            ot[k * 128 : k * 128 + rows, at] = onehot(ub[:rows] == sub[:rows] + k * 128)
        for k in range(3):
            tt[k * 128 : k * 128 + 128, at] = onehot(tb == sub + k * 128)
        uc = jnp.transpose(ub.astype(F32))
        tc = jnp.transpose(tb.astype(F32))
        for k in range(3):
            hit = onehot(uc == lane + float(k * 128))
            o2[at, k * 128 : k * 128 + 128] = hit
            o2[at, E + k * 128 : E + k * 128 + 128] = hit
            hit = onehot(tc == lane + float(k * 128))
            t2[at, k * 128 : k * 128 + 128] = hit
            t2[at, E + k * 128 : E + k * 128 + 128] = hit
        for k in range(2):
            hit = onehot(uc == lane + float(E + k * 128))
            oh2[at, k * 128 : k * 128 + 128] = hit
            oh2[at, 256 + k * 128 : 256 + k * 128 + 128] = hit
        return carry

    lax.fori_loop(0, TILES, tile, 0)
    position = lax.broadcasted_iota(I32, (1, E), 1)
    group = (position >= HALO).astype(I32) + (position >= 2 * HALO).astype(I32) + (position >= 3 * HALO).astype(I32)
    partner_row = rev[...] + group * HALO
    for k in range(3):
        pb = jnp.broadcast_to(partner_row[:, k * 128 : k * 128 + 128], (128, 128))
        pc = jnp.transpose(pb.astype(F32))
        for i in range(3):
            rt[i * 128 : i * 128 + 128, k * 128 : k * 128 + 128] = onehot(pb == sub + i * 128)
            r[k * 128 : k * 128 + 128, i * 128 : i * 128 + 128] = onehot(pc == lane + float(i * 128))
    row = lax.broadcasted_iota(I32, (1, D), 1)
    j = jnp.bitwise_xor(row >> 1, me[0])
    place = ((j & 1) << 8) + (flip2(j >> 1) << 6) + (flip2(j >> 6) << 4) + (flip3(j >> 3) << 1) + (row & 1)
    pick[...] = onehot(jnp.broadcast_to(place, (D, D)) == lax.broadcasted_iota(I32, (D, D), 0))
    high, low = split(m[...])
    m2[:E], m2[E:] = high, low
    high, low = split(coeffs[...])
    c3[:16], c3[16:32], c3[32:] = high, high, low
    high, low = split(wb[...])
    w3[:16], w3[16:32], w3[32:] = high, low, high

    def gather(i, carry):
        at = pl.ds(pl.multiple_of(i * CHUNK, CHUNK), CHUNK)
        tw[at, :] = tn(c3[:, at], w3[...])
        gath[at, :] = nn(o2[at, :], m2[...])
        return carry

    lax.fori_loop(0, SLOTS // CHUNK, gather, 0)
    wr_hi[...], wr_lo[...] = split(wr[...])
    for l in range(2):
        wl_hi[l], wl_lo[l] = split(wl[l])


def slope(v, s):
    return s * (1.0 + v * (1.0 - s))


def middle(
    halo_a, halo_b, a0, a1, a2, a3, m, cot, gath0, tw, oh2, t2, tt, r, rt, pick, coeffs,
    wr_hi, wr_lo, wl_hi, wl_lo,
    out, gmp, gr, wt_hi, wt_lo, own, send,
    h2, gath, th, tl, g2, p, c_s, rm_hi, rm_lo, hs_hi, hs_lo, gp_hi, gp_lo,
):
    scale = float(98304) ** -0.5
    high, low = split(halo_a[...])
    h2[:96], h2[256:352] = high, low
    high, low = split(halo_b[...])
    h2[96:192], h2[352:448] = high, low
    h2[192:256] = jnp.zeros((64, D), BF16)
    h2[448:512] = jnp.zeros((64, D), BF16)

    def finish(i, carry):
        at = pl.ds(pl.multiple_of(i * CHUNK, CHUNK), CHUNK)
        full = gath0[at, :] + nn(oh2[at, :], h2[...])
        gath[at, :] = full
        th[at, :], tl[at, :] = split(full * tw[at, :])
        return carry

    lax.fori_loop(0, SLOTS // CHUNK, finish, 0)
    agg = nn(tt[...], th[...]) + nn(tt[...], tl[...])
    arrived = jnp.concatenate([a0[...], a1[...], a2[...], a3[...]], axis=0)
    high, low = split(arrived)
    rm_hi[...] = nn(r[...], high).astype(BF16)
    rm_lo[...] = nn(r[...], low).astype(BF16)
    w_rev = (wr_hi[...], wr_lo[...])
    rp = dot3(nn, (rm_hi[...], rm_lo[...]), w_rev)
    rs = jax.nn.sigmoid(rp)
    gate = rp * rs
    h = m[...] + agg + m[...] * gate
    pre, sig = [], []
    for l in range(2):
        hs_hi[l], hs_lo[l] = split(h)
        v = dot3(nn, (hs_hi[l], hs_lo[l]), (wl_hi[l], wl_lo[l]))
        s = jax.nn.sigmoid(v)
        pre.append(v)
        sig.append(s)
        h = h + v * s
    out[...] = h
    g = cot[...]
    for l in (1, 0):
        gp_hi[l], gp_lo[l] = split(g * slope(pre[l], sig[l]))
        g = g + dot3(nt, (gp_hi[l], gp_lo[l]), (wl_hi[l], wl_lo[l]))
    gmp[...] = g * (1.0 + gate)
    gp_hi[2], gp_lo[2] = split(g * m[...] * slope(rp, rs))
    q = (nn(rt[...], gp_hi[2]).astype(BF16), nn(rt[...], gp_lo[2]).astype(BF16))
    gr[...] = dot3(nt, q, w_rev)
    g2[:E], g2[E:] = split(g)

    def back(i, carry):
        at = pl.ds(pl.multiple_of(i * CHUNK, CHUNK), CHUNK)
        prod = nn(t2[at, :], g2[...])
        p[0, at, :], p[1, at, :] = split(prod * gath[at, :])
        wt_hi[at, :], wt_lo[at, :] = split(prod * tw[at, :])
        return carry

    lax.fori_loop(0, SLOTS // CHUNK, back, 0)
    c_hi, c_lo = split(coeffs[...])
    c_s[:16], c_s[16:] = c_hi, c_lo
    both = nn(c_s[...], p[0])
    basis = (both[:16] + both[16:] + nn(c_s[:16], p[1])) * scale
    for ref in (own, send):
        ref[256:264, :512] = basis[:8]
        ref[256:264, 512:1024] = basis[8:]
        ref[256:264, 1024:] = jnp.zeros((8, 512), F32)
    for k in range(3):
        left = (hs_hi[k], hs_lo[k]) if k < 2 else (rm_hi[...], rm_lo[...])
        left = (nt(pick[...], left[0]).astype(BF16), nt(pick[...], left[1]).astype(BF16))
        gw = dot3(nn, left, (gp_hi[k], gp_lo[k])) * scale
        own[:256, k * D : k * D + D] = gw[:256]
        send[:256, k * D : k * D + D] = gw[256:]


def scatter(ot, wt_hi, wt_lo, gmp, gm, rim_a, rim_b):
    rims = nn(ot[E:, :], wt_hi[...]) + nn(ot[E:, :], wt_lo[...])
    rim_a[...] = rims[:HALO]
    rim_b[...] = rims[HALO:]
    gm[...] = gmp[...] + (nn(ot[:E, :], wt_hi[...]) + nn(ot[:E, :], wt_lo[...]))


def finish(gm, g0, g1, g2, g3, from_prev, from_next, out):
    for k, ref in enumerate((g0, g1, g2, g3)):
        at = pl.ds(k * HALO, HALO)
        total = gm[at, :] + ref[...]
        if k == 0:
            total = total + from_prev[...]
        if k == 3:
            total = total + from_next[...]
        out[at, :] = total


def call(kernel, outs, n_scalar, n_in, scratch=(), flops=0, grant=60):
    vmem, smem = pl.BlockSpec(memory_space=pltpu.VMEM), pl.BlockSpec(memory_space=pltpu.SMEM)
    return pl.pallas_call(
        kernel,
        out_shape=[jax.ShapeDtypeStruct(shape, dtype) for shape, dtype in outs],
        in_specs=[smem] * n_scalar + [vmem] * n_in,
        out_specs=[vmem] * len(outs),
        scratch_shapes=list(scratch),
        compiler_params=pltpu.CompilerParams(vmem_limit_bytes=grant << 20),
        cost_estimate=pl.CostEstimate(flops=flops, bytes_accessed=8 << 20, transcendentals=0),
    )


def swap(value, mask):
    count = lax.axis_size("edges")
    return lax.ppermute(value, "edges", [(i, i ^ mask) for i in range(count)])


def shift(value, by):
    count = lax.axis_size("edges")
    return lax.ppermute(value, "edges", [(i, (i + by) % count) for i in range(count)])


REV_BITS = (0, 2, 5, 7)


def halve(rows, extra, axis, mask):
    columns = rows.shape[-1]
    keep = lax.index_in_dim(rows, 0, axis, keepdims=False)
    give = lax.index_in_dim(rows, 1, axis, keepdims=False)
    sent = jnp.concatenate([give.reshape(-1, columns), extra], axis=0)
    got = swap(sent, mask)
    n = got.shape[0] - 8
    return keep + got[:n].reshape(keep.shape), extra + got[n:]


def on_device(messages, rev_slot, tri_basis, tri_source, tri_target, tile_block, tile_count, w_basis, w_rev, w_layers, cotangent):
    me = lax.axis_index("edges").astype(I32).reshape(1)
    arrived = [swap(messages[k * HALO : k * HALO + HALO], 1 << b) for k, b in enumerate(REV_BITS)]
    halo_b = shift(messages[E - HALO :], 1)
    halo_a = shift(messages[:HALO], -1)
    (gath0, tw, oh2, ot, t2, tt, r, rt, pick, wr_hi, wr_lo, wl_hi, wl_lo) = call(
        prepare,
        [
            ((SLOTS, D), F32), ((SLOTS, D), F32), ((SLOTS, 512), BF16), ((WIN, SLOTS), BF16),
            ((SLOTS, 2 * E), BF16), ((E, SLOTS), BF16), ((E, E), BF16), ((E, E), BF16), ((D, D), BF16),
            ((D, D), BF16), ((D, D), BF16), ((2, D, D), BF16), ((2, D, D), BF16),
        ],
        3, 8,
        [
            pltpu.VMEM((SLOTS, 2 * E), BF16), pltpu.VMEM((2 * E, D), BF16),
            pltpu.VMEM((48, SLOTS), BF16), pltpu.VMEM((48, D), BF16),
        ],
        flops=4_000_000_000,
        grant=40,
    )(
        me, tile_count, tile_block, tri_source.reshape(1, SLOTS), tri_target.reshape(1, SLOTS),
        rev_slot.reshape(1, E), tri_basis, w_basis, messages, w_rev, w_layers,
    )
    out, gmp, gr, wt_hi, wt_lo, own, send = call(
        middle,
        [
            ((E, D), F32), ((E, D), F32), ((E, D), F32), ((SLOTS, D), BF16), ((SLOTS, D), BF16),
            ((264, 3 * D), F32), ((264, 3 * D), F32),
        ],
        0, 21,
        [
            pltpu.VMEM((512, D), BF16), pltpu.VMEM((SLOTS, D), F32),
            pltpu.VMEM((SLOTS, D), BF16), pltpu.VMEM((SLOTS, D), BF16),
            pltpu.VMEM((2 * E, D), BF16), pltpu.VMEM((2, SLOTS, D), BF16), pltpu.VMEM((32, SLOTS), BF16),
            pltpu.VMEM((E, D), BF16), pltpu.VMEM((E, D), BF16),
            pltpu.VMEM((2, E, D), BF16), pltpu.VMEM((2, E, D), BF16),
            pltpu.VMEM((3, E, D), BF16), pltpu.VMEM((3, E, D), BF16),
        ],
        flops=16_000_000_000,
    )(halo_a, halo_b, *arrived, messages, cotangent, gath0, tw, oh2, t2, tt, r, rt, pick, tri_basis, wr_hi, wr_lo, wl_hi, wl_lo)
    got = swap(send, 1)
    back = [swap(gr[k * HALO : k * HALO + HALO], 1 << b) for k, b in enumerate(REV_BITS)]
    gm, rim_a, rim_b = call(
        scatter, [((E, D), F32), ((HALO, D), F32), ((HALO, D), F32)], 0, 4, flops=4_000_000_000, grant=30
    )(ot, wt_hi, wt_lo, gmp)
    from_prev = shift(rim_a, 1)
    from_next = shift(rim_b, -1)
    total = own + got
    rows, extra = total[:256], total[256:]
    a, b = rows[:, :768].reshape(2, 2, 2, 2, 16, 768), rows[:, 768:].reshape(2, 2, 2, 2, 16, 768)
    ea, eb = extra[:, :768], extra[:, 768:]
    a, ea = halve(a, ea, 0, 2)
    b, eb = halve(b, eb, 2, 64)
    a, ea = halve(a, ea, 0, 4)
    b, eb = halve(b, eb, 2, 128)
    a, ea = halve(a, ea, 0, 64)
    b, eb = halve(b, eb, 0, 2)
    a, ea = halve(a, ea, 0, 128)
    b, eb = halve(b, eb, 0, 4)
    c = jnp.concatenate([a, b], axis=-1).reshape(2, 2, 2, 2, 3 * D)
    ec = jnp.concatenate([ea, eb], axis=-1)
    c, ec = halve(c, ec, 0, 8)
    c, ec = halve(c, ec, 0, 16)
    c, ec = halve(c, ec, 0, 32)
    grads = c.reshape(2, 3, D).transpose(1, 0, 2).reshape(3, 2 * D)
    grad_basis = jnp.concatenate([ec[:, :D], ec[:, D : 2 * D]], axis=0)
    (grad_messages,) = call(finish, [((E, D), F32)], 0, 7, flops=1_000_000, grant=10)(
        gm, *back, from_prev, from_next
    )
    return (out, grad_messages, grads[:2], grads[2], grad_basis)


def solution(mesh):
    split_rows, flat = P("edges", None), P("edges")
    in_specs = (split_rows, flat, P(None, "edges"), flat, flat, flat, flat, P(), P(), P(), split_rows)
    out_specs = (split_rows, split_rows, P(None, "edges"), flat, P())
    return jax.shard_map(on_device, mesh=mesh, in_specs=in_specs, out_specs=out_specs, check_vma=False)
```

```python
import jax
import jax.numpy as jnp
from jax import lax
from jax.experimental import pallas as pl
from jax.experimental.pallas import tpu as pltpu
from jax.sharding import PartitionSpec as P


F32, BF16, I32 = jnp.float32, jnp.bfloat16, jnp.int32
D, E, HALO, SLOTS, TILES = 512, 384, 96, 1536, 12
WIN = E + 2 * HALO
PAD = 640
HALF = 768
CHUNK = 512


def split(value):
    high = value.astype(BF16)
    return high, (value - high.astype(F32)).astype(BF16)


def nn(a, b):
    return lax.dot_general(a, b, (((1,), (0,)), ((), ())), preferred_element_type=F32)


def nt(a, b):
    return lax.dot_general(a, b, (((1,), (1,)), ((), ())), preferred_element_type=F32)


def tn(a, b):
    return lax.dot_general(a, b, (((0,), (0,)), ((), ())), preferred_element_type=F32)


def dot3(op, a, b):
    return op(a[0], b[0]) + (op(a[1], b[0]) + op(a[0], b[1]))


def onehot(values, base, lanes):
    shifted = (values - float(base)).astype(BF16)
    return jnp.where(shifted == lanes, jnp.ones_like(lanes), jnp.zeros_like(lanes))


def prepare(
    me, count, blocks, ints, coeffs, wb, m, core_in, side_in, wr, wl,
    gath, tw, agg, ot, t2, r, rt, pick, wr_hi, wr_lo, wl_hi, wl_lo,
    ow, w2, tt, th, tl, c3, w3, wr_s, wl_s, sem,
):
    copies = [pltpu.make_async_copy(wr, wr_s, sem.at[0]), pltpu.make_async_copy(wl, wl_s, sem.at[1])]
    for copy in copies:
        copy.start()
    lane = lax.broadcasted_iota(I32, (128, 128), 1).astype(F32).astype(BF16)
    sub = lax.broadcasted_iota(I32, (128, 128), 0).astype(F32).astype(BF16)
    n_live = count[0]
    odd = me[0] & 1

    def tile(j, carry):
        start = pl.multiple_of(j * 128, 128)
        at = pl.ds(start, 128)
        w = ints[:, at]
        low = w + (E + HALO) - HALO * odd
        high = w - HALO * (1 - odd)
        u = jnp.where(w < HALO, low, jnp.where(w >= E + HALO, high, w - HALO))
        t = ints[:, pl.ds(pl.multiple_of(SLOTS + j * 128, 128), 128)] + blocks[j] * 128
        t = jnp.where(j < n_live, t, -1)
        ub = jnp.broadcast_to(u.astype(F32), (128, 128))
        tb = jnp.broadcast_to(t.astype(F32), (128, 128))
        for k in range(5):
            rows = 128 if k < 4 else 64
            ot[k * 128 : k * 128 + rows, at] = onehot(ub, k * 128, sub)[:rows]
        for k in range(3):
            tt[k * 128 : k * 128 + 128, at] = onehot(tb, k * 128, sub)
        uc = jnp.transpose(ub)
        tc = jnp.transpose(tb)
        for k in range(5):
            hit = onehot(uc, k * 128, lane)
            ow[at, k * 128 : k * 128 + 128] = hit
            ow[at, PAD + k * 128 : PAD + k * 128 + 128] = hit
        for k in range(3):
            hit = onehot(tc, k * 128, lane)
            t2[at, k * 128 : k * 128 + 128] = hit
            t2[at, E + k * 128 : E + k * 128 + 128] = hit
        return carry

    lax.fori_loop(0, TILES, tile, 0)
    position = lax.broadcasted_iota(I32, (1, E), 1)
    group = (position >= HALO).astype(I32) + (position >= 2 * HALO).astype(I32) + (position >= 3 * HALO).astype(I32)
    partner_row = (ints[:, 2 * SLOTS :] + group * HALO).astype(F32)
    for k in range(3):
        pb = jnp.broadcast_to(partner_row[:, k * 128 : k * 128 + 128], (128, 128))
        pc = jnp.transpose(pb)
        for i in range(3):
            rt[i * 128 : i * 128 + 128, k * 128 : k * 128 + 128] = onehot(pb, i * 128, sub)
            r[k * 128 : k * 128 + 128, i * 128 : i * 128 + 128] = onehot(pc, i * 128, lane)
    row = lax.broadcasted_iota(I32, (1, D), 1)
    j = jnp.bitwise_xor(row >> 1, me[0])
    bit = [(j >> b) & 1 for b in range(8)]
    order = [
        bit[0], bit[1] ^ bit[2], bit[2], bit[6] ^ bit[7], bit[7], bit[3], bit[4] ^ bit[5], bit[5], row & 1,
    ]
    place = order[0]
    for b in order[1:]:
        place = 2 * place + b
    hits = jnp.broadcast_to(place, (D, D)) == lax.broadcasted_iota(I32, (D, D), 0)
    pick[...] = jnp.where(hits, 1.0, 0.0).astype(BF16)
    for at, rows, source in ((0, E, m[...]), (E, HALO, core_in[HALO:, :]), (E + HALO, HALO, side_in[...])):
        w2[at : at + rows], w2[PAD + at : PAD + at + rows] = split(source)
    w2[WIN:PAD] = jnp.zeros((PAD - WIN, D), BF16)
    w2[PAD + WIN :] = jnp.zeros((PAD - WIN, D), BF16)
    high, low = split(coeffs[...])
    c3[:16], c3[16:32], c3[32:] = high, high, low
    high, low = split(wb[...])
    w3[:16], w3[16:32], w3[32:] = high, low, high

    def gather(i, carry):
        at = pl.ds(pl.multiple_of(i * CHUNK, CHUNK), CHUNK)
        weight = tn(c3[:, at], w3[...])
        rows = nn(ow[at, :], w2[...])
        tw[at, :] = weight
        gath[at, :] = rows
        th[at, :], tl[at, :] = split(rows * weight)
        return carry

    lax.fori_loop(0, SLOTS // CHUNK, gather, 0)
    agg[...] = nn(tt[...], th[...]) + nn(tt[...], tl[...])
    for copy in copies:
        copy.wait()
    wr_hi[...], wr_lo[...] = split(wr_s[...])
    for l in range(2):
        wl_hi[l], wl_lo[l] = split(wl_s[l])


def slope(v, s):
    return s * (1.0 + v * (1.0 - s))


def middle(
    core_in, a1, a2, a3, m, cot, gath, tw, agg, t2, r, rt, pick, coeffs, wr_hi, wr_lo, wl_hi, wl_lo,
    out, gmp, gr0, gr1, gr2, gr3, wt_hi, wt_lo, own, send,
    g2, p, c_s, rm_hi, rm_lo, hs_hi, hs_lo, gp_hi, gp_lo,
):
    scale = float(98304) ** -0.5
    arrived = jnp.concatenate([core_in[:HALO, :], a1[...], a2[...], a3[...]], axis=0)
    high, low = split(arrived)
    rm_hi[...] = nn(r[...], high).astype(BF16)
    rm_lo[...] = nn(r[...], low).astype(BF16)
    w_rev = (wr_hi[...], wr_lo[...])
    rp = dot3(nn, (rm_hi[...], rm_lo[...]), w_rev)
    rs = jax.nn.sigmoid(rp)
    gate = rp * rs
    h = m[...] + agg[...] + m[...] * gate
    pre, sig = [], []
    for l in range(2):
        hs_hi[l], hs_lo[l] = split(h)
        v = dot3(nn, (hs_hi[l], hs_lo[l]), (wl_hi[l], wl_lo[l]))
        s = jax.nn.sigmoid(v)
        pre.append(v)
        sig.append(s)
        h = h + v * s
    out[...] = h
    g = cot[...]
    for l in (1, 0):
        gp_hi[l], gp_lo[l] = split(g * slope(pre[l], sig[l]))
        g = g + dot3(nt, (gp_hi[l], gp_lo[l]), (wl_hi[l], wl_lo[l]))
    gmp[...] = g * (1.0 + gate)
    gp_hi[2], gp_lo[2] = split(g * m[...] * slope(rp, rs))
    q = (nn(rt[...], gp_hi[2]).astype(BF16), nn(rt[...], gp_lo[2]).astype(BF16))
    rows = dot3(nt, q, w_rev)
    for k, ref in enumerate((gr0, gr1, gr2, gr3)):
        ref[...] = rows[k * HALO : k * HALO + HALO]
    g2[:E], g2[E:] = split(g)

    def back(i, carry):
        at = pl.ds(pl.multiple_of(i * CHUNK, CHUNK), CHUNK)
        prod = nn(t2[at, :], g2[...])
        p[0, at, :], p[1, at, :] = split(prod * gath[at, :])
        wt_hi[at, :], wt_lo[at, :] = split(prod * tw[at, :])
        return carry

    lax.fori_loop(0, SLOTS // CHUNK, back, 0)
    c_s[:16], c_s[16:] = split(coeffs[...])
    both = nn(c_s[...], p[0])
    basis = (both[:16] + both[16:] + nn(c_s[:16], p[1])) * scale
    for ref in (own, send):
        ref[256:264, :512] = basis[:8]
        ref[256:264, 512:1024] = basis[8:]
        ref[256:264, 1024:] = jnp.zeros((8, 512), F32)
    for k in range(3):
        left = (hs_hi[k], hs_lo[k]) if k < 2 else (rm_hi[...], rm_lo[...])
        left = (nt(pick[...], left[0]).astype(BF16), nt(pick[...], left[1]).astype(BF16))
        gw = dot3(nn, left, (gp_hi[k], gp_lo[k])) * scale
        straight = HALF - k * D if k < 2 else 0
        straight = min(max(straight, 0), D)
        for half, ref in ((0, own), (256, send)):
            if straight:
                ref[:256, k * D : k * D + straight] = gw[half : half + 256, :straight]
            if straight < D:
                for x in range(4):
                    for y in range(4):
                        ref[(y * 4 + x) * 16 : (y * 4 + x) * 16 + 16, k * D + straight : k * D + D] = gw[
                            half + (x * 4 + y) * 16 : half + (x * 4 + y) * 16 + 16, straight:
                        ]


def scatter(ot, wt_hi, wt_lo, gmp, gr0, gm, core_out, side_out):
    rims = nn(ot[E:, :], wt_hi[...]) + nn(ot[E:, :], wt_lo[...])
    core_out[:HALO] = gr0[...]
    core_out[HALO:] = rims[:HALO]
    side_out[...] = rims[HALO:]
    gm[...] = gmp[...] + (nn(ot[:E, :], wt_hi[...]) + nn(ot[:E, :], wt_lo[...]))


def finish(me, gm, core_in, g1, g2, g3, side_in, out):
    odd = me[0] & 1
    out[:HALO] = gm[:HALO] + core_in[:HALO]
    for k, ref in enumerate((g1, g2, g3)):
        at = slice((k + 1) * HALO, (k + 2) * HALO)
        out[at] = gm[at] + ref[...]
    last = E - HALO
    at = pl.ds(pl.multiple_of(last * (1 - odd), 32), HALO)
    out[at, :] = out[at, :] + core_in[HALO:]
    at = pl.ds(pl.multiple_of(last * odd, 32), HALO)
    out[at, :] = out[at, :] + side_in[...]


def halves(rows, extra, keep, send):
    n = rows.shape[0] // 2
    keep[...] = rows[:n]
    send[:n] = rows[n:]
    send[n:] = extra


def fold_core(own, got, keep_a, send_a, keep_b, send_b):
    for at, keep, send in ((slice(0, HALF), keep_a, send_a), (slice(HALF, 2 * HALF), keep_b, send_b)):
        halves(own[:256, at] + got[:256, at], own[256:, at] + got[256:, at], keep, send)


def fold(keep, send, got, keep_next, send_next):
    n = keep.shape[0]
    halves(keep[...] + got[:n], send[n:] + got[n:], keep_next, send_next)


def fold_join(keep_a, send_a, got_a, keep_b, send_b, got_b, keep_next, send_next):
    n = keep_a.shape[0]
    for at, keep, send, got in ((slice(0, HALF), keep_a, send_a, got_a), (slice(HALF, 2 * HALF), keep_b, send_b, got_b)):
        rows = keep[...] + got[:n]
        keep_next[:, at] = rows[: n // 2]
        send_next[: n // 2, at] = rows[n // 2 :]
        send_next[n // 2 :, at] = send[n:] + got[n:]


def fold_last(keep, send, got, layers, rev, basis):
    rows = keep[...] + got[:2]
    extra = send[2:] + got[2:]
    for k in range(3):
        for a in range(2):
            piece = rows[a : a + 1, k * D : k * D + D]
            if k < 2:
                layers[k : k + 1, a * D : a * D + D] = piece
            else:
                rev[:, a * D : a * D + D] = piece
    basis[:8] = extra[:, :D]
    basis[8:] = extra[:, D : 2 * D]


def call(kernel, outs, specs, scratch=(), flops=1_000_000, grant=8):
    places = {
        "s": pl.BlockSpec(memory_space=pltpu.SMEM),
        "v": pl.BlockSpec(memory_space=pltpu.VMEM),
        "h": pl.BlockSpec(memory_space=pl.ANY),
    }
    return pl.pallas_call(
        kernel,
        out_shape=[jax.ShapeDtypeStruct(shape, dtype) for shape, dtype in outs],
        in_specs=[places[c] for c in specs],
        out_specs=[places["v"]] * len(outs),
        scratch_shapes=list(scratch),
        compiler_params=pltpu.CompilerParams(vmem_limit_bytes=grant << 20),
        cost_estimate=pl.CostEstimate(flops=flops, bytes_accessed=1 << 20, transcendentals=0),
    )


def swap(value, mask):
    count = lax.axis_size("edges")
    return lax.ppermute(value, "edges", [(i, i ^ mask) for i in range(count)])


def swap_side(value):
    count = lax.axis_size("edges")
    return lax.ppermute(value, "edges", [(i, (i + (1 if i % 2 else -1)) % count) for i in range(count)])


def tie(value, *others):
    return lax.optimization_barrier((value, *others))[0]


def step(state, got):
    keep, send = state
    n, columns = keep.shape
    return call(fold, [((n // 2, columns), F32), ((n // 2 + 8, columns), F32)], "vvv")(keep, send, got)


def on_device(messages, rev_slot, tri_basis, tri_source, tri_target, tile_block, tile_count, w_basis, w_rev, w_layers, cotangent):
    index = lax.axis_index("edges").astype(I32)
    me = index.reshape(1)
    odd = index & 1
    toward_core = lax.dynamic_slice_in_dim(messages, (E - HALO) * (1 - odd), HALO)
    toward_side = lax.dynamic_slice_in_dim(messages, (E - HALO) * odd, HALO)
    side_in = swap_side(toward_side)
    core_in = swap(jnp.concatenate([messages[:HALO], toward_core], axis=0), 1)
    a2 = swap(messages[2 * HALO : 3 * HALO], 32)
    a3 = swap(messages[3 * HALO :], 128)
    a1 = swap(messages[HALO : 2 * HALO], 4)
    ints = jnp.concatenate([tri_source, tri_target, rev_slot]).reshape(1, 2 * SLOTS + E)
    (gath, tw, agg, ot, t2, r, rt, pick, wr_hi, wr_lo, wl_hi, wl_lo) = call(
        prepare,
        [
            ((SLOTS, D), F32), ((SLOTS, D), F32), ((E, D), F32), ((WIN, SLOTS), BF16), ((SLOTS, 2 * E), BF16),
            ((E, E), BF16), ((E, E), BF16), ((D, D), BF16),
            ((D, D), BF16), ((D, D), BF16), ((2, D, D), BF16), ((2, D, D), BF16),
        ],
        "sss" + "v" * 6 + "hh",
        [
            pltpu.VMEM((SLOTS, 2 * PAD), BF16), pltpu.VMEM((2 * PAD, D), BF16), pltpu.VMEM((E, SLOTS), BF16),
            pltpu.VMEM((SLOTS, D), BF16), pltpu.VMEM((SLOTS, D), BF16),
            pltpu.VMEM((48, SLOTS), BF16), pltpu.VMEM((48, D), BF16),
            pltpu.VMEM((D, D), F32), pltpu.VMEM((2, D, D), F32), pltpu.SemaphoreType.DMA((2,)),
        ],
        flops=4_000_000_000,
        grant=26,
    )(me, tile_count, tile_block, ints, tri_basis, w_basis, messages, core_in, side_in, w_rev, w_layers)
    quarter = ((HALO, D), F32)
    out, gmp, gr0, gr1, gr2, gr3, wt_hi, wt_lo, own, send = call(
        middle,
        [
            ((E, D), F32), ((E, D), F32), quarter, quarter, quarter, quarter,
            ((SLOTS, D), BF16), ((SLOTS, D), BF16), ((264, 3 * D), F32), ((264, 3 * D), F32),
        ],
        "v" * 18,
        [
            pltpu.VMEM((2 * E, D), BF16), pltpu.VMEM((2, SLOTS, D), BF16), pltpu.VMEM((32, SLOTS), BF16),
            pltpu.VMEM((E, D), BF16), pltpu.VMEM((E, D), BF16),
            pltpu.VMEM((2, E, D), BF16), pltpu.VMEM((2, E, D), BF16),
            pltpu.VMEM((3, E, D), BF16), pltpu.VMEM((3, E, D), BF16),
        ],
        flops=16_000_000_000,
        grant=16,
    )(core_in, a1, a2, a3, messages, cotangent, gath, tw, agg, t2, r, rt, pick, tri_basis, wr_hi, wr_lo, wl_hi, wl_lo)

    got = swap(send, 1)
    b2 = swap(gr2, 32)
    gm, core_out, side_out = call(
        scatter, [((E, D), F32), ((2 * HALO, D), F32), quarter], "v" * 5, flops=1_000_000_000, grant=6
    )(ot, wt_hi, wt_lo, gmp, gr0)
    keep_a, send_a, keep_b, send_b = call(
        fold_core, [((128, HALF), F32), ((136, HALF), F32), ((128, HALF), F32), ((136, HALF), F32)], "vv"
    )(own, got)
    a, b = (keep_a, send_a), (keep_b, send_b)
    got_a, got_b = swap(a[1], 2), swap(b[1], 64)
    core_back = swap(core_out, 1)
    side_back = swap_side(side_out)
    got_b = tie(got_b, gm, core_out, side_out, b2)
    a, b = step(a, got_a), step(b, got_b)
    b1 = swap(tie(gr1, got_b), 4)
    got_a, got_b = swap(a[1], 6), swap(b[1], 192)
    got_b = tie(got_b, core_back, side_back)
    a, b = step(a, got_a), step(b, got_b)
    b3 = swap(tie(gr3, got_b), 128)
    got_a, got_b = swap(a[1], 64), swap(b[1], 2)
    got_b = tie(got_b, b1)
    a, b = step(a, got_a), step(b, got_b)
    got_a, got_b = swap(a[1], 192), swap(b[1], 6)
    got_b = tie(got_b, b3)
    c = call(fold_join, [((8, 3 * D), F32), ((16, 3 * D), F32)], "v" * 6)(*a, got_a, *b, got_b)
    got = swap(c[1], 8)
    (grad_messages,) = call(finish, [((E, D), F32)], "s" + "v" * 6)(me, gm, core_back, b1, b2, b3, side_back)
    got = tie(got, grad_messages)
    c = step(c, got)
    c = step(c, swap(c[1], 16))
    layers, rev, basis = call(fold_last, [((2, 2 * D), F32), ((1, 2 * D), F32), ((16, D), F32)], "vvv")(
        *c, swap(c[1], 48)
    )
    return (out, grad_messages, layers, rev.reshape(2 * D), basis)


def solution(mesh):
    split_rows, flat = P("edges", None), P("edges")
    in_specs = (split_rows, flat, P(None, "edges"), flat, flat, flat, flat, P(), P(), P(), split_rows)
    out_specs = (split_rows, split_rows, P(None, "edges"), flat, P())
    return jax.shard_map(on_device, mesh=mesh, in_specs=in_specs, out_specs=out_specs, check_vma=False)
```

```python
import jax
import jax.numpy as jnp
from jax import lax
from jax.experimental import pallas as pl
from jax.experimental.pallas import tpu as pltpu
from jax.sharding import PartitionSpec as P


F32, BF16, I32 = jnp.float32, jnp.bfloat16, jnp.int32
D, E, HALO, SLOTS, TILES = 512, 384, 96, 1536, 12
WIN = E + 2 * HALO
PAD = 640
HALF = 768
CHUNK = 512


def split(value):
    high = value.astype(BF16)
    return high, (value - high.astype(F32)).astype(BF16)


def nn(a, b):
    return lax.dot_general(a, b, (((1,), (0,)), ((), ())), preferred_element_type=F32)


def nt(a, b):
    return lax.dot_general(a, b, (((1,), (1,)), ((), ())), preferred_element_type=F32)


def tn(a, b):
    return lax.dot_general(a, b, (((0,), (0,)), ((), ())), preferred_element_type=F32)


def dot3(op, a, b):
    return op(a[0], b[0]) + (op(a[1], b[0]) + op(a[0], b[1]))


def onehot(values, base, lanes):
    shifted = (values - float(base)).astype(BF16)
    return jnp.where(shifted == lanes, jnp.ones_like(lanes), jnp.zeros_like(lanes))


def prepare(
    me, count, blocks, ints, coeffs, wb, m, core_in, side_in, wl,
    gath, tw, agg, ot, t2, r, rt, pick, wl_hi, wl_lo,
    ow, w2, tt, th, tl, c3, w3, wl_s, sem,
):
    copy = pltpu.make_async_copy(wl, wl_s, sem)
    copy.start()
    lane = lax.broadcasted_iota(I32, (128, 128), 1).astype(F32).astype(BF16)
    sub = lax.broadcasted_iota(I32, (128, 128), 0).astype(F32).astype(BF16)
    n_live = count[0]
    odd = me[0] & 1

    def tile(j, carry):
        start = pl.multiple_of(j * 128, 128)
        at = pl.ds(start, 128)
        w = ints[:, at]
        low = w + (E + HALO) - HALO * odd
        high = w - HALO * (1 - odd)
        u = jnp.where(w < HALO, low, jnp.where(w >= E + HALO, high, w - HALO))
        t = ints[:, pl.ds(pl.multiple_of(SLOTS + j * 128, 128), 128)] + blocks[j] * 128
        t = jnp.where(j < n_live, t, -1)
        ub = jnp.broadcast_to(u.astype(F32), (128, 128))
        tb = jnp.broadcast_to(t.astype(F32), (128, 128))
        for k in range(5):
            rows = 128 if k < 4 else 64
            ot[k * 128 : k * 128 + rows, at] = onehot(ub, k * 128, sub)[:rows]
        for k in range(3):
            tt[k * 128 : k * 128 + 128, at] = onehot(tb, k * 128, sub)
        uc = jnp.transpose(ub)
        tc = jnp.transpose(tb)
        for k in range(5):
            hit = onehot(uc, k * 128, lane)
            ow[at, k * 128 : k * 128 + 128] = hit
            ow[at, PAD + k * 128 : PAD + k * 128 + 128] = hit
        for k in range(3):
            hit = onehot(tc, k * 128, lane)
            t2[at, k * 128 : k * 128 + 128] = hit
            t2[at, E + k * 128 : E + k * 128 + 128] = hit
        return carry

    lax.fori_loop(0, TILES, tile, 0)
    position = lax.broadcasted_iota(I32, (1, E), 1)
    group = (position >= HALO).astype(I32) + (position >= 2 * HALO).astype(I32) + (position >= 3 * HALO).astype(I32)
    partner_row = (ints[:, 2 * SLOTS :] + group * HALO).astype(F32)
    for k in range(3):
        pb = jnp.broadcast_to(partner_row[:, k * 128 : k * 128 + 128], (128, 128))
        pc = jnp.transpose(pb)
        for i in range(3):
            rt[i * 128 : i * 128 + 128, k * 128 : k * 128 + 128] = onehot(pb, i * 128, sub)
            r[k * 128 : k * 128 + 128, i * 128 : i * 128 + 128] = onehot(pc, i * 128, lane)
    row = lax.broadcasted_iota(I32, (1, D), 1)
    j = jnp.bitwise_xor(row >> 1, me[0])
    bit = [(j >> b) & 1 for b in range(8)]
    order = [
        bit[0], bit[1] ^ bit[2], bit[2], bit[6] ^ bit[7], bit[7], bit[3], bit[4] ^ bit[5], bit[5], row & 1,
    ]
    place = order[0]
    for b in order[1:]:
        place = 2 * place + b
    hits = jnp.broadcast_to(place, (D, D)) == lax.broadcasted_iota(I32, (D, D), 0)
    pick[...] = jnp.where(hits, 1.0, 0.0).astype(BF16)
    for at, rows, source in ((0, E, m[...]), (E, HALO, core_in[HALO:, :]), (E + HALO, HALO, side_in[...])):
        w2[at : at + rows], w2[PAD + at : PAD + at + rows] = split(source)
    w2[WIN:PAD] = jnp.zeros((PAD - WIN, D), BF16)
    w2[PAD + WIN :] = jnp.zeros((PAD - WIN, D), BF16)
    high, low = split(coeffs[...])
    c3[:16], c3[16:32], c3[32:] = high, high, low
    high, low = split(wb[...])
    w3[:16], w3[16:32], w3[32:] = high, low, high

    def gather(i, carry):
        at = pl.ds(pl.multiple_of(i * CHUNK, CHUNK), CHUNK)
        weight = tn(c3[:, at], w3[...])
        rows = nn(ow[at, :], w2[...])
        tw[at, :] = weight
        gath[at, :] = rows
        th[at, :], tl[at, :] = split(rows * weight)
        return carry

    lax.fori_loop(0, SLOTS // CHUNK, gather, 0)
    agg[...] = nn(tt[...], th[...]) + nn(tt[...], tl[...])
    copy.wait()
    for l in range(2):
        wl_hi[l], wl_lo[l] = split(wl_s[l])


def slope(v, s):
    return s * (1.0 + v * (1.0 - s))


def middle(
    core_in, a1, a2, a3, m, cot, gath, tw, agg, t2, r, rt, pick, coeffs, wr, wl_hi, wl_lo,
    out, gmp, gr0, gr1, gr2, gr3, wt_hi, wt_lo, own, send,
    wr_hi, wr_lo, g2, p, c_s, rm_hi, rm_lo, hs_hi, hs_lo, gp_hi, gp_lo,
):
    scale = float(98304) ** -0.5
    arrived = jnp.concatenate([core_in[:HALO, :], a1[...], a2[...], a3[...]], axis=0)
    high, low = split(arrived)
    rm_hi[...] = nn(r[...], high).astype(BF16)
    rm_lo[...] = nn(r[...], low).astype(BF16)
    wr_hi[...], wr_lo[...] = split(wr[...])
    w_rev = (wr_hi[...], wr_lo[...])
    rp = dot3(nn, (rm_hi[...], rm_lo[...]), w_rev)
    rs = jax.nn.sigmoid(rp)
    gate = rp * rs
    h = m[...] + agg[...] + m[...] * gate
    pre, sig = [], []
    for l in range(2):
        hs_hi[l], hs_lo[l] = split(h)
        v = dot3(nn, (hs_hi[l], hs_lo[l]), (wl_hi[l], wl_lo[l]))
        s = jax.nn.sigmoid(v)
        pre.append(v)
        sig.append(s)
        h = h + v * s
    out[...] = h
    g = cot[...]
    for l in (1, 0):
        gp_hi[l], gp_lo[l] = split(g * slope(pre[l], sig[l]))
        g = g + dot3(nt, (gp_hi[l], gp_lo[l]), (wl_hi[l], wl_lo[l]))
    gmp[...] = g * (1.0 + gate)
    gp_hi[2], gp_lo[2] = split(g * m[...] * slope(rp, rs))
    q = (nn(rt[...], gp_hi[2]).astype(BF16), nn(rt[...], gp_lo[2]).astype(BF16))
    rows = dot3(nt, q, w_rev)
    for k, ref in enumerate((gr0, gr1, gr2, gr3)):
        ref[...] = rows[k * HALO : k * HALO + HALO]
    g2[:E], g2[E:] = split(g)

    def back(i, carry):
        at = pl.ds(pl.multiple_of(i * CHUNK, CHUNK), CHUNK)
        prod = nn(t2[at, :], g2[...])
        p[0, at, :], p[1, at, :] = split(prod * gath[at, :])
        wt_hi[at, :], wt_lo[at, :] = split(prod * tw[at, :])
        return carry

    lax.fori_loop(0, SLOTS // CHUNK, back, 0)
    c_s[:16], c_s[16:] = split(coeffs[...])
    both = nn(c_s[...], p[0])
    basis = (both[:16] + both[16:] + nn(c_s[:16], p[1])) * scale
    for ref in (own, send):
        ref[256:264, :512] = basis[:8]
        ref[256:264, 512:1024] = basis[8:]
        ref[256:264, 1024:] = jnp.zeros((8, 512), F32)
    for k in range(3):
        left = (hs_hi[k], hs_lo[k]) if k < 2 else (rm_hi[...], rm_lo[...])
        left = (nt(pick[...], left[0]).astype(BF16), nt(pick[...], left[1]).astype(BF16))
        gw = dot3(nn, left, (gp_hi[k], gp_lo[k])) * scale
        straight = HALF - k * D if k < 2 else 0
        straight = min(max(straight, 0), D)
        for half, ref in ((0, own), (256, send)):
            if straight:
                ref[:256, k * D : k * D + straight] = gw[half : half + 256, :straight]
            if straight < D:
                for x in range(4):
                    for y in range(4):
                        ref[(y * 4 + x) * 16 : (y * 4 + x) * 16 + 16, k * D + straight : k * D + D] = gw[
                            half + (x * 4 + y) * 16 : half + (x * 4 + y) * 16 + 16, straight:
                        ]


def scatter(ot, wt_hi, wt_lo, gmp, gr0, gm, core_out, side_out):
    rims = nn(ot[E:, :], wt_hi[...]) + nn(ot[E:, :], wt_lo[...])
    core_out[:HALO] = gr0[...]
    core_out[HALO:] = rims[:HALO]
    side_out[...] = rims[HALO:]
    gm[...] = gmp[...] + (nn(ot[:E, :], wt_hi[...]) + nn(ot[:E, :], wt_lo[...]))


def finish(me, gm, core_in, g1, g2, g3, side_in, out):
    odd = me[0] & 1
    out[:HALO] = gm[:HALO] + core_in[:HALO]
    for k, ref in enumerate((g1, g2, g3)):
        at = slice((k + 1) * HALO, (k + 2) * HALO)
        out[at] = gm[at] + ref[...]
    last = E - HALO
    at = pl.ds(pl.multiple_of(last * (1 - odd), 32), HALO)
    out[at, :] = out[at, :] + core_in[HALO:]
    at = pl.ds(pl.multiple_of(last * odd, 32), HALO)
    out[at, :] = out[at, :] + side_in[...]


def halves(rows, extra, keep, send):
    n = rows.shape[0] // 2
    keep[...] = rows[:n]
    send[:n] = rows[n:]
    send[n:] = extra


def fold_core(own, got, keep_a, send_a, keep_b, send_b):
    for at, keep, send in ((slice(0, HALF), keep_a, send_a), (slice(HALF, 2 * HALF), keep_b, send_b)):
        halves(own[:256, at] + got[:256, at], own[256:, at] + got[256:, at], keep, send)


def fold(keep, send, got, keep_next, send_next):
    n = keep.shape[0]
    halves(keep[...] + got[:n], send[n:] + got[n:], keep_next, send_next)


def fold_join(keep_a, send_a, got_a, keep_b, send_b, got_b, keep_next, send_next):
    n = keep_a.shape[0]
    for at, keep, send, got in ((slice(0, HALF), keep_a, send_a, got_a), (slice(HALF, 2 * HALF), keep_b, send_b, got_b)):
        rows = keep[...] + got[:n]
        keep_next[:, at] = rows[: n // 2]
        send_next[: n // 2, at] = rows[n // 2 :]
        send_next[n // 2 :, at] = send[n:] + got[n:]


def fold_last(keep, send, got, layers, rev, basis):
    rows = keep[...] + got[:2]
    extra = send[2:] + got[2:]
    for k in range(3):
        for a in range(2):
            piece = rows[a : a + 1, k * D : k * D + D]
            if k < 2:
                layers[k : k + 1, a * D : a * D + D] = piece
            else:
                rev[:, a * D : a * D + D] = piece
    basis[:8] = extra[:, :D]
    basis[8:] = extra[:, D : 2 * D]


def call(kernel, outs, specs, scratch=(), flops=1_000_000, grant=8):
    places = {
        "s": pl.BlockSpec(memory_space=pltpu.SMEM),
        "v": pl.BlockSpec(memory_space=pltpu.VMEM),
        "h": pl.BlockSpec(memory_space=pltpu.HBM),
    }
    return pl.pallas_call(
        kernel,
        out_shape=[jax.ShapeDtypeStruct(shape, dtype) for shape, dtype in outs],
        in_specs=[places[c] for c in specs],
        out_specs=[places["v"]] * len(outs),
        scratch_shapes=list(scratch),
        compiler_params=pltpu.CompilerParams(vmem_limit_bytes=grant << 20),
        cost_estimate=pl.CostEstimate(flops=flops, bytes_accessed=1 << 20, transcendentals=0),
    )


def swap(value, mask):
    count = lax.axis_size("edges")
    return lax.ppermute(value, "edges", [(i, i ^ mask) for i in range(count)])


def swap_side(value):
    count = lax.axis_size("edges")
    return lax.ppermute(value, "edges", [(i, (i + (1 if i % 2 else -1)) % count) for i in range(count)])


def tie(value, *others):
    return lax.optimization_barrier((value, *others))[0]


def step(state, got):
    keep, send = state
    n, columns = keep.shape
    return call(fold, [((n // 2, columns), F32), ((n // 2 + 8, columns), F32)], "vvv")(keep, send, got)


def on_device_body(messages, rev_slot, tri_basis, tri_source, tri_target, tile_block, tile_count, w_basis, w_rev, w_layers, cotangent):
    index = lax.axis_index("edges").astype(I32)
    me = index.reshape(1)
    odd = index & 1
    toward_core = lax.dynamic_slice_in_dim(messages, (E - HALO) * (1 - odd), HALO)
    toward_side = lax.dynamic_slice_in_dim(messages, (E - HALO) * odd, HALO)
    a2 = swap(messages[2 * HALO : 3 * HALO], 32)
    side_in = swap_side(toward_side)
    core_in = swap(jnp.concatenate([messages[:HALO], toward_core], axis=0), 1)
    a3 = swap(messages[3 * HALO :], 128)
    a1 = swap(messages[HALO : 2 * HALO], 4)
    ints = jnp.concatenate([tri_source, tri_target, rev_slot]).reshape(1, 2 * SLOTS + E)
    (gath, tw, agg, ot, t2, r, rt, pick, wl_hi, wl_lo) = call(
        prepare,
        [
            ((SLOTS, D), F32), ((SLOTS, D), F32), ((E, D), F32), ((WIN, SLOTS), BF16), ((SLOTS, 2 * E), BF16),
            ((E, E), BF16), ((E, E), BF16), ((D, D), BF16),
            ((2, D, D), BF16), ((2, D, D), BF16),
        ],
        "sss" + "v" * 6 + "h",
        [
            pltpu.VMEM((SLOTS, 2 * PAD), BF16), pltpu.VMEM((2 * PAD, D), BF16), pltpu.VMEM((E, SLOTS), BF16),
            pltpu.VMEM((SLOTS, D), BF16), pltpu.VMEM((SLOTS, D), BF16),
            pltpu.VMEM((48, SLOTS), BF16), pltpu.VMEM((48, D), BF16),
            pltpu.VMEM((2, D, D), F32), pltpu.SemaphoreType.DMA,
        ],
        flops=4_000_000_000,
        grant=26,
    )(me, tile_count, tile_block, ints, tri_basis, w_basis, messages, core_in, side_in, w_layers)
    quarter = ((HALO, D), F32)
    out, gmp, gr0, gr1, gr2, gr3, wt_hi, wt_lo, own, send = call(
        middle,
        [
            ((E, D), F32), ((E, D), F32), quarter, quarter, quarter, quarter,
            ((SLOTS, D), BF16), ((SLOTS, D), BF16), ((264, 3 * D), F32), ((264, 3 * D), F32),
        ],
        "v" * 17,
        [
            pltpu.VMEM((D, D), BF16), pltpu.VMEM((D, D), BF16),
            pltpu.VMEM((2 * E, D), BF16), pltpu.VMEM((2, SLOTS, D), BF16), pltpu.VMEM((32, SLOTS), BF16),
            pltpu.VMEM((E, D), BF16), pltpu.VMEM((E, D), BF16),
            pltpu.VMEM((2, E, D), BF16), pltpu.VMEM((2, E, D), BF16),
            pltpu.VMEM((3, E, D), BF16), pltpu.VMEM((3, E, D), BF16),
        ],
        flops=16_000_000_000,
        grant=16,
    )(core_in, a1, a2, a3, messages, cotangent, gath, tw, agg, t2, r, rt, pick, tri_basis, w_rev, wl_hi, wl_lo)

    got = swap(send, 1)
    b2 = swap(gr2, 32)
    gm, core_out, side_out = call(
        scatter, [((E, D), F32), ((2 * HALO, D), F32), quarter], "v" * 5, flops=1_000_000_000, grant=6
    )(ot, wt_hi, wt_lo, gmp, gr0)
    core_back = swap(core_out, 1)
    side_back = swap_side(side_out)
    b1 = swap(gr1, 4)
    b3 = swap(gr3, 128)
    (grad_messages,) = call(finish, [((E, D), F32)], "s" + "v" * 6)(me, gm, core_back, b1, b2, b3, side_back)
    keep_a, send_a, keep_b, send_b = call(
        fold_core, [((128, HALF), F32), ((136, HALF), F32), ((128, HALF), F32), ((136, HALF), F32)], "vv"
    )(own, got)
    a, b = (keep_a, send_a), (keep_b, send_b)
    for mask_a, mask_b in ((2, 64), (6, 192), (64, 2)):
        got_a, got_b = swap(a[1], mask_a), swap(b[1], mask_b)
        a, b = step(a, got_a), step(b, got_b)
    got_a, got_b = swap(a[1], 192), swap(b[1], 6)
    c = call(fold_join, [((8, 3 * D), F32), ((16, 3 * D), F32)], "v" * 6)(*a, got_a, *b, got_b)
    c = step(c, swap(c[1], 8))
    c = step(c, swap(c[1], 16))
    got = tie(swap(c[1], 48), grad_messages)
    layers, rev, basis = call(fold_last, [((2, 2 * D), F32), ((1, 2 * D), F32), ((16, D), F32)], "vvv")(*c, got)
    return (out, grad_messages, layers, rev.reshape(2 * D), basis)


def solution(mesh):
    split_rows, flat = P("edges", None), P("edges")
    in_specs = (split_rows, flat, P(None, "edges"), flat, flat, flat, flat, P(), P(), P(), split_rows)
    out_specs = (split_rows, split_rows, P(None, "edges"), flat, P())
    return jax.shard_map(on_device_body, mesh=mesh, in_specs=in_specs, out_specs=out_specs, check_vma=False)
```

```python
import jax
import jax.numpy as jnp
from jax import lax
from jax.experimental import pallas as pl
from jax.experimental.pallas import tpu as pltpu
from jax.sharding import PartitionSpec as P


F32, BF16, I32 = jnp.float32, jnp.bfloat16, jnp.int32
D, E, HALO, SLOTS, TILES = 512, 384, 96, 1536, 12
WIN = E + 2 * HALO
PAD = 640
HALF, PART = 768, 384
CHUNK = 512


def split(value):
    high = value.astype(BF16)
    return high, (value - high.astype(F32)).astype(BF16)


def nn(a, b):
    return lax.dot_general(a, b, (((1,), (0,)), ((), ())), preferred_element_type=F32)


def nt(a, b):
    return lax.dot_general(a, b, (((1,), (1,)), ((), ())), preferred_element_type=F32)


def tn(a, b):
    return lax.dot_general(a, b, (((0,), (0,)), ((), ())), preferred_element_type=F32)


def dot3(op, a, b):
    return op(a[0], b[0]) + (op(a[1], b[0]) + op(a[0], b[1]))


def onehot(values, base, lanes):
    shifted = (values - float(base)).astype(BF16)
    return jnp.where(shifted == lanes, jnp.ones_like(lanes), jnp.zeros_like(lanes))


def prepare(
    me, count, blocks, ints, coeffs, wb, m, core_in, side_in, wl,
    gath, tw, agg, ot, t2, r, rt, pick, wl_hi, wl_lo,
    ow, w2, tt, th, tl, c3, w3, wl_s, sem,
):
    copy = pltpu.make_async_copy(wl, wl_s, sem)
    copy.start()
    lane = lax.broadcasted_iota(I32, (128, 128), 1).astype(F32).astype(BF16)
    sub = lax.broadcasted_iota(I32, (128, 128), 0).astype(F32).astype(BF16)
    n_live = count[0]
    odd = me[0] & 1

    def tile(j, carry):
        start = pl.multiple_of(j * 128, 128)
        at = pl.ds(start, 128)
        w = ints[:, at]
        low = w + (E + HALO) - HALO * odd
        high = w - HALO * (1 - odd)
        u = jnp.where(w < HALO, low, jnp.where(w >= E + HALO, high, w - HALO))
        t = ints[:, pl.ds(pl.multiple_of(SLOTS + j * 128, 128), 128)] + blocks[j] * 128
        t = jnp.where(j < n_live, t, -1)
        ub = jnp.broadcast_to(u.astype(F32), (128, 128))
        tb = jnp.broadcast_to(t.astype(F32), (128, 128))
        for k in range(5):
            rows = 128 if k < 4 else 64
            ot[k * 128 : k * 128 + rows, at] = onehot(ub, k * 128, sub)[:rows]
        for k in range(3):
            tt[k * 128 : k * 128 + 128, at] = onehot(tb, k * 128, sub)
        uc = jnp.transpose(ub)
        tc = jnp.transpose(tb)
        for k in range(5):
            hit = onehot(uc, k * 128, lane)
            ow[at, k * 128 : k * 128 + 128] = hit
            ow[at, PAD + k * 128 : PAD + k * 128 + 128] = hit
        for k in range(3):
            hit = onehot(tc, k * 128, lane)
            t2[at, k * 128 : k * 128 + 128] = hit
            t2[at, E + k * 128 : E + k * 128 + 128] = hit
        return carry

    lax.fori_loop(0, TILES, tile, 0)
    position = lax.broadcasted_iota(I32, (1, E), 1)
    group = (position >= HALO).astype(I32) + (position >= 2 * HALO).astype(I32) + (position >= 3 * HALO).astype(I32)
    partner_row = (ints[:, 2 * SLOTS :] + group * HALO).astype(F32)
    for k in range(3):
        pb = jnp.broadcast_to(partner_row[:, k * 128 : k * 128 + 128], (128, 128))
        pc = jnp.transpose(pb)
        for i in range(3):
            rt[i * 128 : i * 128 + 128, k * 128 : k * 128 + 128] = onehot(pb, i * 128, sub)
            r[k * 128 : k * 128 + 128, i * 128 : i * 128 + 128] = onehot(pc, i * 128, lane)
    row = lax.broadcasted_iota(I32, (1, D), 1)
    j = jnp.bitwise_xor(row >> 1, me[0])
    bit = [(j >> b) & 1 for b in range(8)]
    order = [
        bit[0], bit[1] ^ bit[2], bit[2], bit[6] ^ bit[7], bit[7], bit[3], bit[4] ^ bit[5], bit[5], row & 1,
    ]
    place = order[0]
    for b in order[1:]:
        place = 2 * place + b
    hits = jnp.broadcast_to(place, (D, D)) == lax.broadcasted_iota(I32, (D, D), 0)
    pick[...] = jnp.where(hits, 1.0, 0.0).astype(BF16)
    for at, rows, source in ((0, E, m[...]), (E, HALO, core_in[HALO:, :]), (E + HALO, HALO, side_in[...])):
        w2[at : at + rows], w2[PAD + at : PAD + at + rows] = split(source)
    w2[WIN:PAD] = jnp.zeros((PAD - WIN, D), BF16)
    w2[PAD + WIN :] = jnp.zeros((PAD - WIN, D), BF16)
    high, low = split(coeffs[...])
    c3[:16], c3[16:32], c3[32:] = high, high, low
    high, low = split(wb[...])
    w3[:16], w3[16:32], w3[32:] = high, low, high

    for i in range(SLOTS // CHUNK):
        at = slice(i * CHUNK, (i + 1) * CHUNK)
        weight = tn(c3[:, at], w3[...])
        rows = nn(ow[at, :], w2[...])
        tw[at, :] = weight
        gath[at, :] = rows
        th[at, :], tl[at, :] = split(rows * weight)
    agg[...] = nn(tt[...], th[...]) + nn(tt[...], tl[...])
    copy.wait()
    for l in range(2):
        wl_hi[l], wl_lo[l] = split(wl_s[l])


def slope(v, s):
    return s * (1.0 + v * (1.0 - s))


def middle(
    core_in, a1, a2, a3, m, cot, gath, tw, agg, t2, r, rt, pick, coeffs, wr, wl_hi, wl_lo,
    out, gmp, gr0, gr1, gr2, gr3, wt_hi, wt_lo, own, send,
    wr_hi, wr_lo, g2, p, c_s, hs, gp_hi, gp_lo, left,
):
    scale = float(98304) ** -0.5
    arrived = jnp.concatenate([core_in[:HALO, :], a1[...], a2[...], a3[...]], axis=0)
    high, low = split(arrived)
    hs[2, :E] = nn(r[...], high).astype(BF16)
    hs[2, E:] = nn(r[...], low).astype(BF16)
    wr_hi[...], wr_lo[...] = split(wr[...])
    w_rev = (wr_hi[...], wr_lo[...])
    rp = dot3(nn, (hs[2, :E], hs[2, E:]), w_rev)
    left[2] = nt(pick[...], hs[2]).astype(BF16)
    rs = jax.nn.sigmoid(rp)
    gate = rp * rs
    h = m[...] + agg[...] + m[...] * gate
    pre, sig = [], []
    for l in range(2):
        hs[l, :E], hs[l, E:] = split(h)
        v = dot3(nn, (hs[l, :E], hs[l, E:]), (wl_hi[l], wl_lo[l]))
        left[l] = nt(pick[...], hs[l]).astype(BF16)
        s = jax.nn.sigmoid(v)
        pre.append(v)
        sig.append(s)
        h = h + v * s
    out[...] = h

    def weight_grad(k):
        gw = (nn(left[k], gp_hi[k]) + nn(left[k, :, :E], gp_lo[k])) * scale
        for half, ref in ((0, own), (256, send)):
            for part in range(4):
                first, last = max(part * PART, k * D), min(part * PART + PART, k * D + D)
                if first >= last:
                    continue
                if part == 0:
                    ref[:256, first:last] = gw[half : half + 256, first - k * D : last - k * D]
                    continue
                for block in range(16):
                    xa, xb, ya, yb = ((block >> b) & 1 for b in (3, 2, 1, 0))
                    to = ((xa, xb, ya, yb), (xb, xa, ya, yb), (ya, yb, xa, xb), (yb, ya, xa, xb))[part]
                    to = 16 * (8 * to[0] + 4 * to[1] + 2 * to[2] + to[3])
                    row = half + 16 * block
                    ref[to : to + 16, first:last] = gw[row : row + 16, first - k * D : last - k * D]

    g = cot[...]
    for l in (1, 0):
        high, low = split(g * slope(pre[l], sig[l]))
        gp_hi[l, :E], gp_hi[l, E:], gp_lo[l] = high, high, low
        g = g + dot3(nt, (gp_hi[l, :E], gp_lo[l]), (wl_hi[l], wl_lo[l]))
        weight_grad(l)
    g2[:E], g2[E:] = split(g)
    gmp[...] = g * (1.0 + gate)
    high, low = split(g * m[...] * slope(rp, rs))
    gp_hi[2, :E], gp_hi[2, E:], gp_lo[2] = high, high, low
    q = (nn(rt[...], gp_hi[2, :E]).astype(BF16), nn(rt[...], gp_lo[2]).astype(BF16))
    rows = dot3(nt, q, w_rev)
    for k, ref in enumerate((gr0, gr1, gr2, gr3)):
        ref[...] = rows[k * HALO : k * HALO + HALO]
    for i in range(SLOTS // CHUNK):
        at = slice(i * CHUNK, (i + 1) * CHUNK)
        prod = nn(t2[at, :], g2[...])
        p[0, at, :], p[1, at, :] = split(prod * gath[at, :])
        wt_hi[at, :], wt_lo[at, :] = split(prod * tw[at, :])
    weight_grad(2)
    c_s[:16], c_s[16:] = split(coeffs[...])
    both = nn(c_s[...], p[0])
    basis = (both[:16] + both[16:] + nn(c_s[:16], p[1])) * scale
    for ref in (own, send):
        ref[256:264, :512] = basis[:8]
        ref[256:264, 512:1024] = basis[8:]
        ref[256:264, 1024:] = jnp.zeros((8, 512), F32)


def scatter(ot, wt_hi, wt_lo, gmp, gr0, gm, core_out, side_out):
    rims = nn(ot[E:, :], wt_hi[...]) + nn(ot[E:, :], wt_lo[...])
    core_out[:HALO] = gr0[...]
    core_out[HALO:] = rims[:HALO]
    side_out[...] = rims[HALO:]
    gm[...] = gmp[...] + (nn(ot[:E, :], wt_hi[...]) + nn(ot[:E, :], wt_lo[...]))


def finish(me, gm, core_in, g1, g2, g3, side_in, out):
    odd = me[0] & 1
    out[:HALO] = gm[:HALO] + core_in[:HALO]
    for k, ref in enumerate((g1, g2, g3)):
        at = slice((k + 1) * HALO, (k + 2) * HALO)
        out[at] = gm[at] + ref[...]
    last = E - HALO
    at = pl.ds(pl.multiple_of(last * (1 - odd), 32), HALO)
    out[at, :] = out[at, :] + core_in[HALO:]
    at = pl.ds(pl.multiple_of(last * odd, 32), HALO)
    out[at, :] = out[at, :] + side_in[...]


def halves(rows, extra, keep, send):
    n = rows.shape[0] // 2
    keep[...] = rows[:n]
    send[:n] = rows[n:]
    send[n:] = extra


def fold_core(own, got, *refs):
    for part in range(4):
        at = slice(part * PART, (part + 1) * PART)
        halves(own[:256, at] + got[:256, at], own[256:, at] + got[256:, at], refs[2 * part], refs[2 * part + 1])


def fold_merge(keep_1, send_1, got_1, keep_2, send_2, got_2, keep_next, send_next):
    n = keep_1.shape[0]
    for at, keep, send, got in ((slice(0, PART), keep_1, send_1, got_1), (slice(PART, HALF), keep_2, send_2, got_2)):
        rows = keep[...] + got[:n]
        keep_next[:, at] = rows[: n // 2]
        send_next[: n // 2, at] = rows[n // 2 :]
        send_next[n // 2 :, at] = send[n:] + got[n:]


def fold(keep, send, got, keep_next, send_next):
    n = keep.shape[0]
    halves(keep[...] + got[:n], send[n:] + got[n:], keep_next, send_next)


def fold_join(keep_a, send_a, got_a, keep_b, send_b, got_b, keep_next, send_1, send_2, send_3):
    n = keep_a.shape[0]
    for at, keep, send, got in ((slice(0, HALF), keep_a, send_a, got_a), (slice(HALF, 2 * HALF), keep_b, send_b, got_b)):
        rows = keep[...] + got[:n]
        extra = send[n:] + got[n:]
        keep_next[:, at] = rows[:4]
        for k, ref in ((8, send_1), (4, send_2), (12, send_3)):
            ref[:4, at] = rows[k : k + 4]
            ref[4:, at] = extra


def fold_four(keep, send, got_1, got_2, got_3, keep_next, send_next):
    rows = (keep[...] + got_2[:4]) + (got_1[:4] + got_3[:4])
    extra = (send[4:] + got_2[4:]) + (got_1[4:] + got_3[4:])
    halves(rows, extra, keep_next, send_next)


def fold_last(keep, send, got, layers, rev, basis):
    rows = keep[...] + got[:2]
    extra = send[2:] + got[2:]
    for k in range(3):
        for a in range(2):
            piece = rows[a : a + 1, k * D : k * D + D]
            if k < 2:
                layers[k : k + 1, a * D : a * D + D] = piece
            else:
                rev[:, a * D : a * D + D] = piece
    basis[:8] = extra[:, :D]
    basis[8:] = extra[:, D : 2 * D]


def call(kernel, outs, specs, scratch=(), flops=1_000_000, grant=8):
    places = {
        "s": pl.BlockSpec(memory_space=pltpu.SMEM),
        "v": pl.BlockSpec(memory_space=pltpu.VMEM),
        "h": pl.BlockSpec(memory_space=pltpu.HBM),
    }
    return pl.pallas_call(
        kernel,
        out_shape=[jax.ShapeDtypeStruct(shape, dtype) for shape, dtype in outs],
        in_specs=[places[c] for c in specs],
        out_specs=[places["v"]] * len(outs),
        scratch_shapes=list(scratch),
        compiler_params=pltpu.CompilerParams(vmem_limit_bytes=grant << 20),
        cost_estimate=pl.CostEstimate(flops=flops, bytes_accessed=1 << 20, transcendentals=0),
    )


def swap(value, mask):
    count = lax.axis_size("edges")
    return lax.ppermute(value, "edges", [(i, i ^ mask) for i in range(count)])


def swap_side(value):
    count = lax.axis_size("edges")
    return lax.ppermute(value, "edges", [(i, (i + (1 if i % 2 else -1)) % count) for i in range(count)])


def tie(value, *others):
    return lax.optimization_barrier((value, *others))[0]


def step(state, got):
    keep, send = state
    n, columns = keep.shape
    return call(fold, [((n // 2, columns), F32), ((n // 2 + 8, columns), F32)], "vvv")(keep, send, got)


def on_device_body(messages, rev_slot, tri_basis, tri_source, tri_target, tile_block, tile_count, w_basis, w_rev, w_layers, cotangent):
    index = lax.axis_index("edges").astype(I32)
    me = index.reshape(1)
    odd = index & 1
    quarter = ((HALO, D), F32)
    toward_core = lax.dynamic_slice_in_dim(messages, (E - HALO) * (1 - odd), HALO)
    toward_side = lax.dynamic_slice_in_dim(messages, (E - HALO) * odd, HALO)
    a2 = swap(messages[2 * HALO : 3 * HALO], 32)
    side_in = swap_side(toward_side)
    core_in = swap(jnp.concatenate([messages[:HALO], toward_core], axis=0), 1)
    a3 = swap(messages[3 * HALO :], 128)
    a1 = swap(messages[HALO : 2 * HALO], 4)
    ints = jnp.concatenate([tri_source, tri_target, rev_slot]).reshape(1, 2 * SLOTS + E)
    (gath, tw, agg, ot, t2, r, rt, pick, wl_hi, wl_lo) = call(
        prepare,
        [
            ((SLOTS, D), F32), ((SLOTS, D), F32), ((E, D), F32), ((WIN, SLOTS), BF16), ((SLOTS, 2 * E), BF16),
            ((E, E), BF16), ((E, E), BF16), ((D, D), BF16),
            ((2, D, D), BF16), ((2, D, D), BF16),
        ],
        "sss" + "v" * 6 + "h",
        [
            pltpu.VMEM((SLOTS, 2 * PAD), BF16), pltpu.VMEM((2 * PAD, D), BF16), pltpu.VMEM((E, SLOTS), BF16),
            pltpu.VMEM((SLOTS, D), BF16), pltpu.VMEM((SLOTS, D), BF16),
            pltpu.VMEM((48, SLOTS), BF16), pltpu.VMEM((48, D), BF16),
            pltpu.VMEM((2, D, D), F32), pltpu.SemaphoreType.DMA,
        ],
        flops=4_000_000_000,
        grant=26,
    )(me, tile_count, tile_block, ints, tri_basis, w_basis, messages, core_in, side_in, w_layers)
    out, gmp, gr0, gr1, gr2, gr3, wt_hi, wt_lo, own, send = call(
        middle,
        [
            ((E, D), F32), ((E, D), F32), quarter, quarter, quarter, quarter,
            ((SLOTS, D), BF16), ((SLOTS, D), BF16), ((264, 3 * D), F32), ((264, 3 * D), F32),
        ],
        "v" * 17,
        [
            pltpu.VMEM((D, D), BF16), pltpu.VMEM((D, D), BF16),
            pltpu.VMEM((2 * E, D), BF16), pltpu.VMEM((2, SLOTS, D), BF16), pltpu.VMEM((32, SLOTS), BF16),
            pltpu.VMEM((3, 2 * E, D), BF16), pltpu.VMEM((3, 2 * E, D), BF16), pltpu.VMEM((3, E, D), BF16),
            pltpu.VMEM((3, D, 2 * E), BF16),
        ],
        flops=16_000_000_000,
        grant=16,
    )(core_in, a1, a2, a3, messages, cotangent, gath, tw, agg, t2, r, rt, pick, tri_basis, w_rev, wl_hi, wl_lo)

    got = swap(send, 1)
    b2 = swap(gr2, 32)
    gm, core_out, side_out = call(
        scatter, [((E, D), F32), ((2 * HALO, D), F32), quarter], "v" * 5, flops=1_000_000_000, grant=6
    )(ot, wt_hi, wt_lo, gmp, gr0)
    core_back = swap(core_out, 1)
    side_back = swap_side(side_out)
    b1 = swap(gr1, 4)
    b3 = swap(gr3, 128)
    (grad_messages,) = call(finish, [((E, D), F32)], "s" + "v" * 6)(me, gm, core_back, b1, b2, b3, side_back)
    parts = call(fold_core, [((128, PART), F32), ((136, PART), F32)] * 4, "vv")(own, got)
    parts = [parts[2 * k : 2 * k + 2] for k in range(4)]
    gots = [swap(part[1], mask) for part, mask in zip(parts, (2, 6, 64, 192))]
    parts = [step(part, arrived) for part, arrived in zip(parts, gots)]
    gots = [swap(part[1], mask) for part, mask in zip(parts, (6, 2, 192, 64))]
    a, b = (
        call(fold_merge, [((32, HALF), F32), ((40, HALF), F32)], "v" * 6)(
            *parts[k], gots[k], *parts[k + 1], gots[k + 1]
        )
        for k in (0, 2)
    )
    got_a, got_b = swap(a[1], 64), swap(b[1], 2)
    a, b = step(a, got_a), step(b, got_b)
    got_a, got_b = swap(a[1], 192), swap(b[1], 6)
    keep, send_1, send_2, send_3 = call(fold_join, [((4, 3 * D), F32)] + [((12, 3 * D), F32)] * 3, "v" * 6)(
        *a, got_a, *b, got_b
    )
    got_1, got_2, got_3 = swap(send_1, 8), swap(send_2, 16), swap(send_3, 24)
    c = call(fold_four, [((2, 3 * D), F32), ((10, 3 * D), F32)], "v" * 5)(keep, send_1, got_1, got_2, got_3)
    got = tie(swap(c[1], 48), grad_messages)
    layers, rev, basis = call(fold_last, [((2, 2 * D), F32), ((1, 2 * D), F32), ((16, D), F32)], "vvv")(*c, got)
    return (out, grad_messages, layers, rev.reshape(2 * D), basis)


def solution(mesh):
    split_rows, flat = P("edges", None), P("edges")
    in_specs = (split_rows, flat, P(None, "edges"), flat, flat, flat, flat, P(), P(), P(), split_rows)
    out_specs = (split_rows, split_rows, P(None, "edges"), flat, P())
    return jax.shard_map(on_device_body, mesh=mesh, in_specs=in_specs, out_specs=out_specs, check_vma=False)
```

```python
import jax
import jax.numpy as jnp
from jax import lax
from jax.experimental import pallas as pl
from jax.experimental.pallas import tpu as pltpu
from jax.sharding import PartitionSpec as P


F32, BF16, I32 = jnp.float32, jnp.bfloat16, jnp.int32
D, E, HALO, SLOTS, TILES = 512, 384, 96, 1536, 12
WIN = E + 2 * HALO
PAD = 640
HALF, PART = 768, 384
CHUNK = 512


def split(value):
    high = value.astype(BF16)
    return high, (value - high.astype(F32)).astype(BF16)


def nn(a, b):
    return lax.dot_general(a, b, (((1,), (0,)), ((), ())), preferred_element_type=F32)


def nt(a, b):
    return lax.dot_general(a, b, (((1,), (1,)), ((), ())), preferred_element_type=F32)


def tn(a, b):
    return lax.dot_general(a, b, (((0,), (0,)), ((), ())), preferred_element_type=F32)


def dot3(op, a, b):
    return op(a[0], b[0]) + (op(a[1], b[0]) + op(a[0], b[1]))


def onehot(values, lanes):
    return jnp.where(values == lanes, jnp.ones_like(lanes), jnp.zeros_like(lanes))


def tall(row):
    return jnp.broadcast_to(row.astype(F32), (128, 128))


def onehots(row, blocks, lane, sub, put_rows, put_columns):
    low, high = row & 127, row >> 7
    base = onehot(tall(low).astype(BF16), sub)
    for k in range(blocks):
        put_rows(k, base * tall(high == k).astype(BF16))
    base = onehot(jnp.transpose(tall(low)).astype(BF16), lane)
    high = jnp.transpose(tall(high)).astype(BF16)
    for k in range(blocks):
        put_columns(k, jnp.where(high == jnp.full_like(high, k), base, jnp.zeros_like(base)))


def prepare(
    me, count, blocks, ints, coeffs, wb, m, core_in, side_in, wl,
    gath, tw, agg, ot, t2, r, rt, pick, wl_hi, wl_lo,
    ow, w2, tt, th, tl, c3, w3, wl_s, sem,
):
    copy = pltpu.make_async_copy(wl, wl_s, sem)
    copy.start()
    lane = lax.broadcasted_iota(I32, (128, 128), 1).astype(F32).astype(BF16)
    sub = lax.broadcasted_iota(I32, (128, 128), 0).astype(F32).astype(BF16)
    n_live = count[0]
    odd = me[0] & 1

    def tile(j, carry):
        start = pl.multiple_of(j * 128, 128)
        at = pl.ds(start, 128)
        w = ints[:, at]
        low = w + (E + HALO) - HALO * odd
        high = w - HALO * (1 - odd)
        u = jnp.where(w < HALO, low, jnp.where(w >= E + HALO, high, w - HALO))
        t = ints[:, pl.ds(pl.multiple_of(SLOTS + j * 128, 128), 128)] + blocks[j] * 128
        t = jnp.where(j < n_live, t, -1)

        def put_ot(k, hit):
            rows = 128 if k < 4 else 64
            ot[k * 128 : k * 128 + rows, at] = hit[:rows]

        def put_ow(k, hit):
            ow[at, k * 128 : k * 128 + 128] = hit
            ow[at, PAD + k * 128 : PAD + k * 128 + 128] = hit

        def put_tt(k, hit):
            tt[k * 128 : k * 128 + 128, at] = hit

        def put_t2(k, hit):
            t2[at, k * 128 : k * 128 + 128] = hit
            t2[at, E + k * 128 : E + k * 128 + 128] = hit

        onehots(u, 5, lane, sub, put_ot, put_ow)
        onehots(t, 3, lane, sub, put_tt, put_t2)
        return carry

    lax.fori_loop(0, TILES, tile, 0)
    position = lax.broadcasted_iota(I32, (1, E), 1)
    group = (position >= HALO).astype(I32) + (position >= 2 * HALO).astype(I32) + (position >= 3 * HALO).astype(I32)
    partner_row = ints[:, 2 * SLOTS :] + group * HALO
    for k in range(3):
        at = slice(k * 128, k * 128 + 128)

        def put_rt(i, hit, at=at):
            rt[i * 128 : i * 128 + 128, at] = hit

        def put_r(i, hit, at=at):
            r[at, i * 128 : i * 128 + 128] = hit

        onehots(partner_row[:, at], 3, lane, sub, put_rt, put_r)
    row = lax.broadcasted_iota(I32, (1, D), 1)
    j = jnp.bitwise_xor(row >> 1, me[0])
    bit = [(j >> b) & 1 for b in range(8)]
    order = [
        bit[0], bit[1] ^ bit[2], bit[2], bit[6] ^ bit[7], bit[7], bit[3], bit[4] ^ bit[5], bit[5], row & 1,
    ]
    place = order[0]
    for b in order[1:]:
        place = 2 * place + b
    hits = jnp.broadcast_to(place, (D, D)) == lax.broadcasted_iota(I32, (D, D), 0)
    pick[...] = jnp.where(hits, 1.0, 0.0).astype(BF16)
    for at, rows, source in ((0, E, m[...]), (E, HALO, core_in[HALO:, :]), (E + HALO, HALO, side_in[...])):
        w2[at : at + rows], w2[PAD + at : PAD + at + rows] = split(source)
    w2[WIN:PAD] = jnp.zeros((PAD - WIN, D), BF16)
    w2[PAD + WIN :] = jnp.zeros((PAD - WIN, D), BF16)
    high, low = split(coeffs[...])
    c3[:16], c3[16:32], c3[32:] = high, high, low
    high, low = split(wb[...])
    w3[:16], w3[16:32], w3[32:] = high, low, high

    for i in range(SLOTS // CHUNK):
        at = slice(i * CHUNK, (i + 1) * CHUNK)
        weight = tn(c3[:, at], w3[...])
        rows = nn(ow[at, :], w2[...])
        tw[at, :] = weight
        gath[at, :] = rows
        th[at, :], tl[at, :] = split(rows * weight)
    agg[...] = nn(tt[...], th[...]) + nn(tt[...], tl[...])
    copy.wait()
    for l in range(2):
        wl_hi[l], wl_lo[l] = split(wl_s[l])


def slope(v, s):
    return s * (1.0 + v * (1.0 - s))


def middle(
    core_in, a1, a2, a3, m, cot, gath, tw, agg, t2, r, rt, pick, coeffs, wr, wl_hi, wl_lo,
    out, gmp, gr0, gr1, gr2, gr3, wt_hi, wt_lo, own, send,
    wr_hi, wr_lo, g2, p, c_s, hs, gp_hi, gp_lo, left,
):
    scale = float(98304) ** -0.5
    arrived = jnp.concatenate([core_in[:HALO, :], a1[...], a2[...], a3[...]], axis=0)
    high, low = split(arrived)
    hs[2, :E] = nn(r[...], high).astype(BF16)
    hs[2, E:] = nn(r[...], low).astype(BF16)
    wr_hi[...], wr_lo[...] = split(wr[...])
    w_rev = (wr_hi[...], wr_lo[...])
    rp = dot3(nn, (hs[2, :E], hs[2, E:]), w_rev)
    left[2] = nt(pick[...], hs[2]).astype(BF16)
    rs = jax.nn.sigmoid(rp)
    gate = rp * rs
    h = m[...] + agg[...] + m[...] * gate
    pre, sig = [], []
    for l in range(2):
        hs[l, :E], hs[l, E:] = split(h)
        v = dot3(nn, (hs[l, :E], hs[l, E:]), (wl_hi[l], wl_lo[l]))
        left[l] = nt(pick[...], hs[l]).astype(BF16)
        s = jax.nn.sigmoid(v)
        pre.append(v)
        sig.append(s)
        h = h + v * s
    out[...] = h

    def weight_grad(k):
        gw = (nn(left[k], gp_hi[k]) + nn(left[k, :, :E], gp_lo[k])) * scale
        for half, ref in ((0, own), (256, send)):
            for part in range(4):
                first, last = max(part * PART, k * D), min(part * PART + PART, k * D + D)
                if first >= last:
                    continue
                if part == 0:
                    ref[:256, first:last] = gw[half : half + 256, first - k * D : last - k * D]
                    continue
                for block in range(16):
                    xa, xb, ya, yb = ((block >> b) & 1 for b in (3, 2, 1, 0))
                    to = ((xa, xb, ya, yb), (xb, xa, ya, yb), (ya, yb, xa, xb), (yb, ya, xa, xb))[part]
                    to = 16 * (8 * to[0] + 4 * to[1] + 2 * to[2] + to[3])
                    row = half + 16 * block
                    ref[to : to + 16, first:last] = gw[row : row + 16, first - k * D : last - k * D]

    g = cot[...]
    for l in (1, 0):
        high, low = split(g * slope(pre[l], sig[l]))
        gp_hi[l, :E], gp_hi[l, E:], gp_lo[l] = high, high, low
        g = g + dot3(nt, (gp_hi[l, :E], gp_lo[l]), (wl_hi[l], wl_lo[l]))
        weight_grad(l)
    g2[:E], g2[E:] = split(g)
    gmp[...] = g * (1.0 + gate)
    high, low = split(g * m[...] * slope(rp, rs))
    gp_hi[2, :E], gp_hi[2, E:], gp_lo[2] = high, high, low
    q = (nn(rt[...], gp_hi[2, :E]).astype(BF16), nn(rt[...], gp_lo[2]).astype(BF16))
    rows = dot3(nt, q, w_rev)
    for k, ref in enumerate((gr0, gr1, gr2, gr3)):
        ref[...] = rows[k * HALO : k * HALO + HALO]
    for i in range(SLOTS // CHUNK):
        at = slice(i * CHUNK, (i + 1) * CHUNK)
        prod = nn(t2[at, :], g2[...])
        p[0, at, :], p[1, at, :] = split(prod * gath[at, :])
        wt_hi[at, :], wt_lo[at, :] = split(prod * tw[at, :])
    weight_grad(2)
    c_s[:16], c_s[16:] = split(coeffs[...])
    both = nn(c_s[...], p[0])
    basis = (both[:16] + both[16:] + nn(c_s[:16], p[1])) * scale
    for ref in (own, send):
        ref[256:264, :512] = basis[:8]
        ref[256:264, 512:1024] = basis[8:]
        ref[256:264, 1024:] = jnp.zeros((8, 512), F32)


def scatter(ot, wt_hi, wt_lo, gmp, gr0, gm, core_out, side_out):
    rims = nn(ot[E:, :], wt_hi[...]) + nn(ot[E:, :], wt_lo[...])
    core_out[:HALO] = gr0[...]
    core_out[HALO:] = rims[:HALO]
    side_out[...] = rims[HALO:]
    gm[...] = gmp[...] + (nn(ot[:E, :], wt_hi[...]) + nn(ot[:E, :], wt_lo[...]))


def finish(me, gm, core_in, g1, g2, g3, side_in, out):
    odd = me[0] & 1
    out[:HALO] = gm[:HALO] + core_in[:HALO]
    for k, ref in enumerate((g1, g2, g3)):
        at = slice((k + 1) * HALO, (k + 2) * HALO)
        out[at] = gm[at] + ref[...]
    last = E - HALO
    at = pl.ds(pl.multiple_of(last * (1 - odd), 32), HALO)
    out[at, :] = out[at, :] + core_in[HALO:]
    at = pl.ds(pl.multiple_of(last * odd, 32), HALO)
    out[at, :] = out[at, :] + side_in[...]


def halves(rows, extra, keep, send):
    n = rows.shape[0] // 2
    keep[...] = rows[:n]
    send[:n] = rows[n:]
    send[n:] = extra


def fold_core(own, got, *refs):
    for part in range(4):
        at = slice(part * PART, (part + 1) * PART)
        halves(own[:256, at] + got[:256, at], own[256:, at] + got[256:, at], refs[2 * part], refs[2 * part + 1])


def fold_merge(keep_1, send_1, got_1, keep_2, send_2, got_2, keep_next, send_next):
    n = keep_1.shape[0]
    for at, keep, send, got in ((slice(0, PART), keep_1, send_1, got_1), (slice(PART, HALF), keep_2, send_2, got_2)):
        rows = keep[...] + got[:n]
        keep_next[:, at] = rows[: n // 2]
        send_next[: n // 2, at] = rows[n // 2 :]
        send_next[n // 2 :, at] = send[n:] + got[n:]


def fold(keep, send, got, keep_next, send_next):
    n = keep.shape[0]
    halves(keep[...] + got[:n], send[n:] + got[n:], keep_next, send_next)


BASIS = 2 * D


def fold_join(keep_a, send_a, got_a, keep_b, send_b, got_b, keep_next, send_next):
    n = keep_a.shape[0]
    for at, keep, send, got in ((0, keep_a, send_a, got_a), (HALF, keep_b, send_b, got_b)):
        rows = keep[...] + got[:n]
        extra = send[n:] + got[n:]
        width = min(HALF, BASIS - at)
        keep_next[:, at : at + HALF] = rows[:8]
        send_next[:, at : at + width] = extra[:, :width]
        send_next[:, BASIS + at : BASIS + at + HALF] = rows[8:]


def fold_z0(keep, send, got, keep_next, send_next):
    rows = keep[...] + got[:, BASIS:]
    keep_next[...] = rows[:4]
    send_next[:, :BASIS] = send[:, :BASIS] + got[:, :BASIS]
    send_next[:4, BASIS:] = rows[4:, :HALF]
    send_next[4:, BASIS:] = rows[4:, HALF:]


def fold_z1(keep, send, got, keep_next, send_next):
    send_next[:, :BASIS] = send[:, :BASIS] + got[:, :BASIS]
    for k in range(2):
        rows = keep[:, k * HALF : k * HALF + HALF] + got[4 * k : 4 * k + 4, BASIS:]
        keep_next[:, k * HALF : k * HALF + HALF] = rows[:2]
        for i in range(2):
            q = 2 * k + i
            send_next[2 * q : 2 * q + 2, BASIS:] = rows[2:, i * PART : i * PART + PART]


def fold_last(keep, send, got, layers, rev, basis):
    extra = send[:, :BASIS] + got[:, :BASIS]
    basis[:8] = extra[:, :D]
    basis[8:] = extra[:, D:]
    for q in range(4):
        rows = keep[:, q * PART : q * PART + PART] + got[2 * q : 2 * q + 2, BASIS:]
        for k in range(3):
            first, last = max(q * PART, k * D), min(q * PART + PART, k * D + D)
            for a in range(2):
                if first < last:
                    piece = rows[a : a + 1, first - q * PART : last - q * PART]
                    at = a * D + first - k * D
                    if k < 2:
                        layers[k : k + 1, at : at + last - first] = piece
                    else:
                        rev[:, at : at + last - first] = piece


def call(kernel, outs, specs, scratch=(), flops=1_000_000, grant=8):
    places = {
        "s": pl.BlockSpec(memory_space=pltpu.SMEM),
        "v": pl.BlockSpec(memory_space=pltpu.VMEM),
        "h": pl.BlockSpec(memory_space=pltpu.HBM),
    }
    return pl.pallas_call(
        kernel,
        out_shape=[jax.ShapeDtypeStruct(shape, dtype) for shape, dtype in outs],
        in_specs=[places[c] for c in specs],
        out_specs=[places["v"]] * len(outs),
        scratch_shapes=list(scratch),
        compiler_params=pltpu.CompilerParams(vmem_limit_bytes=grant << 20),
        cost_estimate=pl.CostEstimate(flops=flops, bytes_accessed=1 << 20, transcendentals=0),
    )


def swap(value, mask):
    count = lax.axis_size("edges")
    return lax.ppermute(value, "edges", [(i, i ^ mask) for i in range(count)])


def swap_side(value):
    count = lax.axis_size("edges")
    return lax.ppermute(value, "edges", [(i, (i + (1 if i % 2 else -1)) % count) for i in range(count)])


def tie(value, *others):
    return lax.optimization_barrier((value, *others))[0]


def step(state, got):
    keep, send = state
    n, columns = keep.shape
    return call(fold, [((n // 2, columns), F32), ((n // 2 + 8, columns), F32)], "vvv")(keep, send, got)


def on_device_body(messages, rev_slot, tri_basis, tri_source, tri_target, tile_block, tile_count, w_basis, w_rev, w_layers, cotangent):
    index = lax.axis_index("edges").astype(I32)
    me = index.reshape(1)
    odd = index & 1
    quarter = ((HALO, D), F32)
    toward_core = lax.dynamic_slice_in_dim(messages, (E - HALO) * (1 - odd), HALO)
    toward_side = lax.dynamic_slice_in_dim(messages, (E - HALO) * odd, HALO)
    a2 = swap(messages[2 * HALO : 3 * HALO], 32)
    side_in = swap_side(toward_side)
    core_in = swap(jnp.concatenate([messages[:HALO], toward_core], axis=0), 1)
    a3 = swap(messages[3 * HALO :], 128)
    a1 = swap(messages[HALO : 2 * HALO], 4)
    ints = jnp.concatenate([tri_source, tri_target, rev_slot]).reshape(1, 2 * SLOTS + E)
    (gath, tw, agg, ot, t2, r, rt, pick, wl_hi, wl_lo) = call(
        prepare,
        [
            ((SLOTS, D), F32), ((SLOTS, D), F32), ((E, D), F32), ((WIN, SLOTS), BF16), ((SLOTS, 2 * E), BF16),
            ((E, E), BF16), ((E, E), BF16), ((D, D), BF16),
            ((2, D, D), BF16), ((2, D, D), BF16),
        ],
        "sss" + "v" * 6 + "h",
        [
            pltpu.VMEM((SLOTS, 2 * PAD), BF16), pltpu.VMEM((2 * PAD, D), BF16), pltpu.VMEM((E, SLOTS), BF16),
            pltpu.VMEM((SLOTS, D), BF16), pltpu.VMEM((SLOTS, D), BF16),
            pltpu.VMEM((48, SLOTS), BF16), pltpu.VMEM((48, D), BF16),
            pltpu.VMEM((2, D, D), F32), pltpu.SemaphoreType.DMA,
        ],
        flops=4_000_000_000,
        grant=26,
    )(me, tile_count, tile_block, ints, tri_basis, w_basis, messages, core_in, side_in, w_layers)
    out, gmp, gr0, gr1, gr2, gr3, wt_hi, wt_lo, own, send = call(
        middle,
        [
            ((E, D), F32), ((E, D), F32), quarter, quarter, quarter, quarter,
            ((SLOTS, D), BF16), ((SLOTS, D), BF16), ((264, 3 * D), F32), ((264, 3 * D), F32),
        ],
        "v" * 17,
        [
            pltpu.VMEM((D, D), BF16), pltpu.VMEM((D, D), BF16),
            pltpu.VMEM((2 * E, D), BF16), pltpu.VMEM((2, SLOTS, D), BF16), pltpu.VMEM((32, SLOTS), BF16),
            pltpu.VMEM((3, 2 * E, D), BF16), pltpu.VMEM((3, 2 * E, D), BF16), pltpu.VMEM((3, E, D), BF16),
            pltpu.VMEM((3, D, 2 * E), BF16),
        ],
        flops=16_000_000_000,
        grant=16,
    )(core_in, a1, a2, a3, messages, cotangent, gath, tw, agg, t2, r, rt, pick, tri_basis, w_rev, wl_hi, wl_lo)

    got = swap(send, 1)
    b2 = swap(gr2, 32)
    gm, core_out, side_out = call(
        scatter, [((E, D), F32), ((2 * HALO, D), F32), quarter], "v" * 5, flops=1_000_000_000, grant=6
    )(ot, wt_hi, wt_lo, gmp, gr0)
    core_back = swap(core_out, 1)
    side_back = swap_side(side_out)
    b1 = swap(gr1, 4)
    b3 = swap(gr3, 128)
    (grad_messages,) = call(finish, [((E, D), F32)], "s" + "v" * 6)(me, gm, core_back, b1, b2, b3, side_back)
    parts = call(fold_core, [((128, PART), F32), ((136, PART), F32)] * 4, "vv")(own, got)
    parts = [parts[2 * k : 2 * k + 2] for k in range(4)]
    gots = [swap(part[1], mask) for part, mask in zip(parts, (2, 6, 64, 192))]
    parts = [step(part, arrived) for part, arrived in zip(parts, gots)]
    gots = [swap(part[1], mask) for part, mask in zip(parts, (6, 2, 192, 64))]
    a, b = (
        call(fold_merge, [((32, HALF), F32), ((40, HALF), F32)], "v" * 6)(
            *parts[k], gots[k], *parts[k + 1], gots[k + 1]
        )
        for k in (0, 2)
    )
    got_a, got_b = swap(a[1], 64), swap(b[1], 2)
    a, b = step(a, got_a), step(b, got_b)
    got_a, got_b = swap(a[1], 192), swap(b[1], 6)
    c = call(fold_join, [((8, 3 * D), F32), ((8, BASIS + 3 * D), F32)], "v" * 6)(*a, got_a, *b, got_b)
    c = call(fold_z0, [((4, 3 * D), F32), ((8, BASIS + HALF), F32)], "vvv")(*c, swap(c[1], 8))
    c = call(fold_z1, [((2, 3 * D), F32), ((8, BASIS + PART), F32)], "vvv")(*c, swap(c[1], 16))
    got = tie(swap(c[1], 48), grad_messages)
    layers, rev, basis = call(fold_last, [((2, 2 * D), F32), ((1, 2 * D), F32), ((16, D), F32)], "vvv")(*c, got)
    return (out, grad_messages, layers, rev.reshape(2 * D), basis)


def solution(mesh):
    split_rows, flat = P("edges", None), P("edges")
    in_specs = (split_rows, flat, P(None, "edges"), flat, flat, flat, flat, P(), P(), P(), split_rows)
    out_specs = (split_rows, split_rows, P(None, "edges"), flat, P())
    return jax.shard_map(on_device_body, mesh=mesh, in_specs=in_specs, out_specs=out_specs, check_vma=False)
```

```python
import jax
import jax.numpy as jnp
from jax import lax
from jax.experimental import pallas as pl
from jax.experimental.pallas import tpu as pltpu
from jax.sharding import PartitionSpec as P


F32, BF16, I32 = jnp.float32, jnp.bfloat16, jnp.int32
D, E, HALO, SLOTS, TILES = 512, 384, 96, 1536, 12
WIN = E + 2 * HALO
PAD = 640
HALF, PART = 768, 384
CHUNK = 512


def split(value):
    high = value.astype(BF16)
    return high, (value - high.astype(F32)).astype(BF16)


def nn(a, b):
    return lax.dot_general(a, b, (((1,), (0,)), ((), ())), preferred_element_type=F32)


def nt(a, b):
    return lax.dot_general(a, b, (((1,), (1,)), ((), ())), preferred_element_type=F32)


def tn(a, b):
    return lax.dot_general(a, b, (((0,), (0,)), ((), ())), preferred_element_type=F32)


def dot3(op, a, b):
    return op(a[0], b[0]) + (op(a[1], b[0]) + op(a[0], b[1]))


def onehot(values, lanes):
    return jnp.where(values == lanes, jnp.ones_like(lanes), jnp.zeros_like(lanes))


def tall(row):
    return jnp.broadcast_to(row.astype(F32), (128, 128))


def onehots(row, blocks, lane, sub, put_rows, put_columns):
    low, high = row & 127, row >> 7
    base = onehot(tall(low).astype(BF16), sub)
    for k in range(blocks):
        put_rows(k, base * tall(high == k).astype(BF16))
    base = onehot(jnp.transpose(tall(low)).astype(BF16), lane)
    high = jnp.transpose(tall(high)).astype(BF16)
    for k in range(blocks):
        put_columns(k, jnp.where(high == jnp.full_like(high, k), base, jnp.zeros_like(base)))


def prepare(
    me, count, blocks, source, target, rev, coeffs, wb, m, core_in, side_in, wl,
    gath, tw, agg, ot, t2, r, rt, pick, wl_hi, wl_lo,
    ints, ow, w2, tt, th, tl, c3, w3, wl_s, sem,
):
    copy = pltpu.make_async_copy(wl, wl_s, sem)
    copy.start()
    ints[:, :SLOTS] = source[...].reshape(1, SLOTS)
    ints[:, SLOTS : 2 * SLOTS] = target[...].reshape(1, SLOTS)
    ints[:, 2 * SLOTS :] = rev[...].reshape(1, E)
    lane = lax.broadcasted_iota(I32, (128, 128), 1).astype(F32).astype(BF16)
    sub = lax.broadcasted_iota(I32, (128, 128), 0).astype(F32).astype(BF16)
    n_live = count[0]
    odd = me[0] & 1

    def tile(j, carry):
        start = pl.multiple_of(j * 128, 128)
        at = pl.ds(start, 128)
        w = ints[:, at]
        low = w + (E + HALO) - HALO * odd
        high = w - HALO * (1 - odd)
        u = jnp.where(w < HALO, low, jnp.where(w >= E + HALO, high, w - HALO))
        t = ints[:, pl.ds(pl.multiple_of(SLOTS + j * 128, 128), 128)] + blocks[j] * 128
        t = jnp.where(j < n_live, t, -1)

        def put_ot(k, hit):
            rows = 128 if k < 4 else 64
            ot[k * 128 : k * 128 + rows, at] = hit[:rows]

        def put_ow(k, hit):
            ow[at, k * 128 : k * 128 + 128] = hit
            ow[at, PAD + k * 128 : PAD + k * 128 + 128] = hit

        def put_tt(k, hit):
            tt[k * 128 : k * 128 + 128, at] = hit

        def put_t2(k, hit):
            t2[at, k * 128 : k * 128 + 128] = hit
            t2[at, E + k * 128 : E + k * 128 + 128] = hit

        onehots(u, 5, lane, sub, put_ot, put_ow)
        onehots(t, 3, lane, sub, put_tt, put_t2)
        return carry

    lax.fori_loop(0, TILES, tile, 0)
    position = lax.broadcasted_iota(I32, (1, E), 1)
    group = (position >= HALO).astype(I32) + (position >= 2 * HALO).astype(I32) + (position >= 3 * HALO).astype(I32)
    partner_row = ints[:, 2 * SLOTS :] + group * HALO
    for k in range(3):
        at = slice(k * 128, k * 128 + 128)

        def put_rt(i, hit, at=at):
            rt[i * 128 : i * 128 + 128, at] = hit

        def put_r(i, hit, at=at):
            r[at, i * 128 : i * 128 + 128] = hit

        onehots(partner_row[:, at], 3, lane, sub, put_rt, put_r)
    row = lax.broadcasted_iota(I32, (1, D), 1)
    j = jnp.bitwise_xor(row >> 1, me[0])
    bit = [(j >> b) & 1 for b in range(8)]
    order = [
        bit[0], bit[1] ^ bit[2], bit[2], bit[6] ^ bit[7], bit[7], bit[3], bit[4] ^ bit[5], bit[5], row & 1,
    ]
    place = order[0]
    for b in order[1:]:
        place = 2 * place + b
    hits = jnp.broadcast_to(place, (D, D)) == lax.broadcasted_iota(I32, (D, D), 0)
    pick[...] = jnp.where(hits, 1.0, 0.0).astype(BF16)
    for at, rows, piece in ((0, E, m[...]), (E, HALO, core_in[HALO:, :]), (E + HALO, HALO, side_in[...])):
        w2[at : at + rows], w2[PAD + at : PAD + at + rows] = split(piece)
    w2[WIN:PAD] = jnp.zeros((PAD - WIN, D), BF16)
    w2[PAD + WIN :] = jnp.zeros((PAD - WIN, D), BF16)
    high, low = split(coeffs[...])
    c3[:16], c3[16:32], c3[32:] = high, high, low
    high, low = split(wb[...])
    w3[:16], w3[16:32], w3[32:] = high, low, high

    for i in range(SLOTS // CHUNK):
        at = slice(i * CHUNK, (i + 1) * CHUNK)
        weight = tn(c3[:, at], w3[...])
        rows = nn(ow[at, :], w2[...])
        tw[at, :] = weight
        gath[at, :] = rows
        th[at, :], tl[at, :] = split(rows * weight)
    agg[...] = nn(tt[...], th[...]) + nn(tt[...], tl[...])
    copy.wait()
    for l in range(2):
        wl_hi[l], wl_lo[l] = split(wl_s[l])


def slope(v, s):
    return s * (1.0 + v * (1.0 - s))


def middle(
    core_in, a1, a2, a3, m, cot, gath, tw, agg, t2, r, rt, pick, coeffs, wr, wl_hi, wl_lo,
    out, gmp, gr0, gr1, gr2, gr3, wt_hi, wt_lo, own, send,
    wr_hi, wr_lo, g2, p, c_s, hs, gp_hi, gp_lo, left,
):
    scale = float(98304) ** -0.5
    arrived = jnp.concatenate([core_in[:HALO, :], a1[...], a2[...], a3[...]], axis=0)
    high, low = split(arrived)
    hs[2, :E] = nn(r[...], high).astype(BF16)
    hs[2, E:] = nn(r[...], low).astype(BF16)
    wr_hi[...], wr_lo[...] = split(wr[...])
    w_rev = (wr_hi[...], wr_lo[...])
    rp = dot3(nn, (hs[2, :E], hs[2, E:]), w_rev)
    left[2] = nt(pick[...], hs[2]).astype(BF16)
    rs = jax.nn.sigmoid(rp)
    gate = rp * rs
    h = m[...] + agg[...] + m[...] * gate
    pre, sig = [], []
    for l in range(2):
        hs[l, :E], hs[l, E:] = split(h)
        v = dot3(nn, (hs[l, :E], hs[l, E:]), (wl_hi[l], wl_lo[l]))
        left[l] = nt(pick[...], hs[l]).astype(BF16)
        s = jax.nn.sigmoid(v)
        pre.append(v)
        sig.append(s)
        h = h + v * s
    out[...] = h

    def weight_grad(k):
        gw = (nn(left[k], gp_hi[k]) + nn(left[k, :, :E], gp_lo[k])) * scale
        for half, ref in ((0, own), (256, send)):
            for part in range(4):
                first, last = max(part * PART, k * D), min(part * PART + PART, k * D + D)
                if first >= last:
                    continue
                if part == 0:
                    ref[:256, first:last] = gw[half : half + 256, first - k * D : last - k * D]
                    continue
                for block in range(16):
                    xa, xb, ya, yb = ((block >> b) & 1 for b in (3, 2, 1, 0))
                    to = ((xa, xb, ya, yb), (xb, xa, ya, yb), (ya, yb, xa, xb), (yb, ya, xa, xb))[part]
                    to = 16 * (8 * to[0] + 4 * to[1] + 2 * to[2] + to[3])
                    row = half + 16 * block
                    ref[to : to + 16, first:last] = gw[row : row + 16, first - k * D : last - k * D]

    g = cot[...]
    for l in (1, 0):
        high, low = split(g * slope(pre[l], sig[l]))
        gp_hi[l, :E], gp_hi[l, E:], gp_lo[l] = high, high, low
        g = g + dot3(nt, (gp_hi[l, :E], gp_lo[l]), (wl_hi[l], wl_lo[l]))
        weight_grad(l)
    g2[:E], g2[E:] = split(g)
    gmp[...] = g * (1.0 + gate)
    high, low = split(g * m[...] * slope(rp, rs))
    gp_hi[2, :E], gp_hi[2, E:], gp_lo[2] = high, high, low
    q = (nn(rt[...], gp_hi[2, :E]).astype(BF16), nn(rt[...], gp_lo[2]).astype(BF16))
    rows = dot3(nt, q, w_rev)
    for k, ref in enumerate((gr0, gr1, gr2, gr3)):
        ref[...] = rows[k * HALO : k * HALO + HALO]
    for i in range(SLOTS // CHUNK):
        at = slice(i * CHUNK, (i + 1) * CHUNK)
        prod = nn(t2[at, :], g2[...])
        p[0, at, :], p[1, at, :] = split(prod * gath[at, :])
        wt_hi[at, :], wt_lo[at, :] = split(prod * tw[at, :])
    weight_grad(2)
    c_s[:16], c_s[16:] = split(coeffs[...])
    both = nn(c_s[...], p[0])
    basis = (both[:16] + both[16:] + nn(c_s[:16], p[1])) * scale
    for ref in (own, send):
        ref[256:264, :512] = basis[:8]
        ref[256:264, 512:1024] = basis[8:]
        ref[256:264, 1024:] = jnp.zeros((8, 512), F32)


def scatter(ot, wt_hi, wt_lo, gmp, gr0, gm, core_out, side_out):
    rims = nn(ot[E:, :], wt_hi[...]) + nn(ot[E:, :], wt_lo[...])
    core_out[:HALO] = gr0[...]
    core_out[HALO:] = rims[:HALO]
    side_out[...] = rims[HALO:]
    gm[...] = gmp[...] + (nn(ot[:E, :], wt_hi[...]) + nn(ot[:E, :], wt_lo[...]))


def finish(me, gm, core_in, g1, g2, g3, side_in, out):
    odd = me[0] & 1
    out[:HALO] = gm[:HALO] + core_in[:HALO]
    for k, ref in enumerate((g1, g2, g3)):
        at = slice((k + 1) * HALO, (k + 2) * HALO)
        out[at] = gm[at] + ref[...]
    last = E - HALO
    at = pl.ds(pl.multiple_of(last * (1 - odd), 32), HALO)
    out[at, :] = out[at, :] + core_in[HALO:]
    at = pl.ds(pl.multiple_of(last * odd, 32), HALO)
    out[at, :] = out[at, :] + side_in[...]


def halves(rows, extra, keep, send):
    n = rows.shape[0] // 2
    keep[...] = rows[:n]
    send[:n] = rows[n:]
    send[n:] = extra


def fold_core(own, got, *refs):
    for part in range(4):
        at = slice(part * PART, (part + 1) * PART)
        halves(own[:256, at] + got[:256, at], own[256:, at] + got[256:, at], refs[2 * part], refs[2 * part + 1])


def fold_merge(keep_1, send_1, got_1, keep_2, send_2, got_2, keep_next, send_next):
    n = keep_1.shape[0]
    for at, keep, send, got in ((slice(0, PART), keep_1, send_1, got_1), (slice(PART, HALF), keep_2, send_2, got_2)):
        rows = keep[...] + got[:n]
        keep_next[:, at] = rows[: n // 2]
        send_next[: n // 2, at] = rows[n // 2 :]
        send_next[n // 2 :, at] = send[n:] + got[n:]


def fold(keep, send, got, keep_next, send_next):
    n = keep.shape[0]
    halves(keep[...] + got[:n], send[n:] + got[n:], keep_next, send_next)


BASIS = 2 * D


def fold_join(keep_a, send_a, got_a, keep_b, send_b, got_b, keep_next, send_next):
    n = keep_a.shape[0]
    for at, keep, send, got in ((0, keep_a, send_a, got_a), (HALF, keep_b, send_b, got_b)):
        rows = keep[...] + got[:n]
        extra = send[n:] + got[n:]
        width = min(HALF, BASIS - at)
        keep_next[:, at : at + HALF] = rows[:8]
        send_next[:, at : at + width] = extra[:, :width]
        send_next[:, BASIS + at : BASIS + at + HALF] = rows[8:]


def fold_z0(keep, send, got, keep_next, send_next):
    rows = keep[...] + got[:, BASIS:]
    keep_next[...] = rows[:4]
    send_next[:, :BASIS] = send[:, :BASIS] + got[:, :BASIS]
    send_next[:4, BASIS:] = rows[4:, :HALF]
    send_next[4:, BASIS:] = rows[4:, HALF:]


def fold_z1(keep, send, got, keep_next, send_next):
    send_next[:, :BASIS] = send[:, :BASIS] + got[:, :BASIS]
    for k in range(2):
        rows = keep[:, k * HALF : k * HALF + HALF] + got[4 * k : 4 * k + 4, BASIS:]
        keep_next[:, k * HALF : k * HALF + HALF] = rows[:2]
        for i in range(2):
            q = 2 * k + i
            send_next[2 * q : 2 * q + 2, BASIS:] = rows[2:, i * PART : i * PART + PART]


def fold_last(keep, send, got, layers, rev, basis):
    extra = send[:, :BASIS] + got[:, :BASIS]
    basis[:8] = extra[:, :D]
    basis[8:] = extra[:, D:]
    for q in range(4):
        rows = keep[:, q * PART : q * PART + PART] + got[2 * q : 2 * q + 2, BASIS:]
        for k in range(3):
            first, last = max(q * PART, k * D), min(q * PART + PART, k * D + D)
            for a in range(2):
                if first < last:
                    piece = rows[a : a + 1, first - q * PART : last - q * PART]
                    at = a * D + first - k * D
                    if k < 2:
                        layers[k : k + 1, at : at + last - first] = piece
                    else:
                        rev[:, at : at + last - first] = piece


def call(kernel, outs, specs, scratch=(), flops=1_000_000, grant=8):
    places = {
        "s": pl.BlockSpec(memory_space=pltpu.SMEM),
        "v": pl.BlockSpec(memory_space=pltpu.VMEM),
        "h": pl.BlockSpec(memory_space=pltpu.HBM),
    }
    return pl.pallas_call(
        kernel,
        out_shape=[jax.ShapeDtypeStruct(shape, dtype) for shape, dtype in outs],
        in_specs=[places[c] for c in specs],
        out_specs=[places["v"]] * len(outs),
        scratch_shapes=list(scratch),
        compiler_params=pltpu.CompilerParams(vmem_limit_bytes=grant << 20),
        cost_estimate=pl.CostEstimate(flops=flops, bytes_accessed=1 << 20, transcendentals=0),
    )


def swap(value, mask):
    count = lax.axis_size("edges")
    return lax.ppermute(value, "edges", [(i, i ^ mask) for i in range(count)])


def swap_side(value):
    count = lax.axis_size("edges")
    return lax.ppermute(value, "edges", [(i, (i + (1 if i % 2 else -1)) % count) for i in range(count)])


def tie(value, *others):
    return lax.optimization_barrier((value, *others))[0]


def step(state, got):
    keep, send = state
    n, columns = keep.shape
    return call(fold, [((n // 2, columns), F32), ((n // 2 + 8, columns), F32)], "vvv")(keep, send, got)


def on_device_body(messages, rev_slot, tri_basis, tri_source, tri_target, tile_block, tile_count, w_basis, w_rev, w_layers, cotangent):
    index = lax.axis_index("edges").astype(I32)
    me = index.reshape(1)
    odd = index & 1
    quarter = ((HALO, D), F32)
    toward_core = lax.dynamic_slice_in_dim(messages, (E - HALO) * (1 - odd), HALO)
    toward_side = lax.dynamic_slice_in_dim(messages, (E - HALO) * odd, HALO)
    a2 = swap(messages[2 * HALO : 3 * HALO], 32)
    side_in = swap_side(toward_side)
    core_in = swap(jnp.concatenate([messages[:HALO], toward_core], axis=0), 1)
    a3 = swap(messages[3 * HALO :], 128)
    a1 = swap(messages[HALO : 2 * HALO], 4)
    (gath, tw, agg, ot, t2, r, rt, pick, wl_hi, wl_lo) = call(
        prepare,
        [
            ((SLOTS, D), F32), ((SLOTS, D), F32), ((E, D), F32), ((WIN, SLOTS), BF16), ((SLOTS, 2 * E), BF16),
            ((E, E), BF16), ((E, E), BF16), ((D, D), BF16),
            ((2, D, D), BF16), ((2, D, D), BF16),
        ],
        "sss" + "v" * 8 + "h",
        [
            pltpu.VMEM((1, 2 * SLOTS + E), I32),
            pltpu.VMEM((SLOTS, 2 * PAD), BF16), pltpu.VMEM((2 * PAD, D), BF16), pltpu.VMEM((E, SLOTS), BF16),
            pltpu.VMEM((SLOTS, D), BF16), pltpu.VMEM((SLOTS, D), BF16),
            pltpu.VMEM((48, SLOTS), BF16), pltpu.VMEM((48, D), BF16),
            pltpu.VMEM((2, D, D), F32), pltpu.SemaphoreType.DMA,
        ],
        flops=4_000_000_000,
        grant=26,
    )(me, tile_count, tile_block, tri_source, tri_target, rev_slot, tri_basis, w_basis, messages, core_in, side_in, w_layers)
    out, gmp, gr0, gr1, gr2, gr3, wt_hi, wt_lo, own, send = call(
        middle,
        [
            ((E, D), F32), ((E, D), F32), quarter, quarter, quarter, quarter,
            ((SLOTS, D), BF16), ((SLOTS, D), BF16), ((264, 3 * D), F32), ((264, 3 * D), F32),
        ],
        "v" * 17,
        [
            pltpu.VMEM((D, D), BF16), pltpu.VMEM((D, D), BF16),
            pltpu.VMEM((2 * E, D), BF16), pltpu.VMEM((2, SLOTS, D), BF16), pltpu.VMEM((32, SLOTS), BF16),
            pltpu.VMEM((3, 2 * E, D), BF16), pltpu.VMEM((3, 2 * E, D), BF16), pltpu.VMEM((3, E, D), BF16),
            pltpu.VMEM((3, D, 2 * E), BF16),
        ],
        flops=16_000_000_000,
        grant=16,
    )(core_in, a1, a2, a3, messages, cotangent, gath, tw, agg, t2, r, rt, pick, tri_basis, w_rev, wl_hi, wl_lo)

    got = swap(send, 1)
    b2 = swap(gr2, 32)
    gm, core_out, side_out = call(
        scatter, [((E, D), F32), ((2 * HALO, D), F32), quarter], "v" * 5, flops=1_000_000_000, grant=6
    )(ot, wt_hi, wt_lo, gmp, gr0)
    core_back = swap(core_out, 1)
    side_back = swap_side(side_out)
    b1 = swap(gr1, 4)
    b3 = swap(gr3, 128)
    (grad_messages,) = call(finish, [((E, D), F32)], "s" + "v" * 6)(me, gm, core_back, b1, b2, b3, side_back)
    parts = call(fold_core, [((128, PART), F32), ((136, PART), F32)] * 4, "vv")(own, got)
    parts = [parts[2 * k : 2 * k + 2] for k in range(4)]
    gots = [swap(part[1], mask) for part, mask in zip(parts, (2, 6, 64, 192))]
    parts = [step(part, arrived) for part, arrived in zip(parts, gots)]
    gots = [swap(part[1], mask) for part, mask in zip(parts, (6, 2, 192, 64))]
    a, b = (
        call(fold_merge, [((32, HALF), F32), ((40, HALF), F32)], "v" * 6)(
            *parts[k], gots[k], *parts[k + 1], gots[k + 1]
        )
        for k in (0, 2)
    )
    got_a, got_b = swap(a[1], 64), swap(b[1], 2)
    a, b = step(a, got_a), step(b, got_b)
    got_a, got_b = swap(a[1], 192), swap(b[1], 6)
    c = call(fold_join, [((8, 3 * D), F32), ((8, BASIS + 3 * D), F32)], "v" * 6)(*a, got_a, *b, got_b)
    c = call(fold_z0, [((4, 3 * D), F32), ((8, BASIS + HALF), F32)], "vvv")(*c, swap(c[1], 8))
    c = call(fold_z1, [((2, 3 * D), F32), ((8, BASIS + PART), F32)], "vvv")(*c, swap(c[1], 16))
    got = tie(swap(c[1], 48), grad_messages)
    layers, rev, basis = call(fold_last, [((2, 2 * D), F32), ((1, 2 * D), F32), ((16, D), F32)], "vvv")(*c, got)
    return (out, grad_messages, layers, rev.reshape(2 * D), basis)


def solution(mesh):
    split_rows, flat = P("edges", None), P("edges")
    in_specs = (split_rows, flat, P(None, "edges"), flat, flat, flat, flat, P(), P(), P(), split_rows)
    out_specs = (split_rows, split_rows, P(None, "edges"), flat, P())
    return jax.shard_map(on_device_body, mesh=mesh, in_specs=in_specs, out_specs=out_specs, check_vma=False)
```

```python
import jax
import jax.numpy as jnp
from jax import lax
from jax.experimental import pallas as pl
from jax.experimental.pallas import tpu as pltpu
from jax.sharding import PartitionSpec as P


F32, BF16, I32 = jnp.float32, jnp.bfloat16, jnp.int32
D, E, HALO, SLOTS, TILES = 512, 384, 96, 1536, 12
WIN = E + 2 * HALO
PAD = 640
HALF, PART = 768, 384
CHUNK = 512


def split(value):
    high = value.astype(BF16)
    return high, (value - high.astype(F32)).astype(BF16)


def nn(a, b):
    return lax.dot_general(a, b, (((1,), (0,)), ((), ())), preferred_element_type=F32)


def nt(a, b):
    return lax.dot_general(a, b, (((1,), (1,)), ((), ())), preferred_element_type=F32)


def tn(a, b):
    return lax.dot_general(a, b, (((0,), (0,)), ((), ())), preferred_element_type=F32)


def dot3(op, a, b):
    return op(a[0], b[0]) + (op(a[1], b[0]) + op(a[0], b[1]))


def onehot(values, lanes):
    return jnp.where(values == lanes, jnp.ones_like(lanes), jnp.zeros_like(lanes))


def tall(row):
    return jnp.broadcast_to(row.astype(F32), (128, 128))


def onehots(row, blocks, lane, sub, put_rows, put_columns):
    low, high = row & 127, row >> 7
    base = onehot(tall(low).astype(BF16), sub)
    for k in range(blocks):
        put_rows(k, base * tall(high == k).astype(BF16))
    base = onehot(jnp.transpose(tall(low)).astype(BF16), lane)
    high = jnp.transpose(tall(high)).astype(BF16)
    for k in range(blocks):
        put_columns(k, jnp.where(high == jnp.full_like(high, k), base, jnp.zeros_like(base)))


def prepare(
    me, count, blocks, source, target, rev, coeffs, wb, m, core_in, side_in, wl,
    gath, tw, agg, ot, t2, r, rt, pick, wl_hi, wl_lo,
    ints, ow, w2, tt, th, tl, c3, w3, wl_s, sem,
):
    copy = pltpu.make_async_copy(wl, wl_s, sem)
    copy.start()
    ints[:, :SLOTS] = source[...].reshape(1, SLOTS)
    ints[:, SLOTS : 2 * SLOTS] = target[...].reshape(1, SLOTS)
    ints[:, 2 * SLOTS :] = rev[...].reshape(1, E)
    lane = lax.broadcasted_iota(I32, (128, 128), 1).astype(F32).astype(BF16)
    sub = lax.broadcasted_iota(I32, (128, 128), 0).astype(F32).astype(BF16)
    n_live = count[0]
    odd = me[0] & 1

    def tile(j, carry):
        start = pl.multiple_of(j * 128, 128)
        at = pl.ds(start, 128)
        w = ints[:, at]
        low = w + (E + HALO) - HALO * odd
        high = w - HALO * (1 - odd)
        u = jnp.where(w < HALO, low, jnp.where(w >= E + HALO, high, w - HALO))
        t = ints[:, pl.ds(pl.multiple_of(SLOTS + j * 128, 128), 128)] + blocks[j] * 128
        t = jnp.where(j < n_live, t, -1)

        def put_ot(k, hit):
            rows = 128 if k < 4 else 64
            ot[k * 128 : k * 128 + rows, at] = hit[:rows]

        def put_ow(k, hit):
            ow[at, k * 128 : k * 128 + 128] = hit
            ow[at, PAD + k * 128 : PAD + k * 128 + 128] = hit

        def put_tt(k, hit):
            tt[k * 128 : k * 128 + 128, at] = hit

        def put_t2(k, hit):
            t2[at, k * 128 : k * 128 + 128] = hit
            t2[at, E + k * 128 : E + k * 128 + 128] = hit

        onehots(u, 5, lane, sub, put_ot, put_ow)
        onehots(t, 3, lane, sub, put_tt, put_t2)
        return carry

    lax.fori_loop(0, TILES, tile, 0)
    position = lax.broadcasted_iota(I32, (1, E), 1)
    group = (position >= HALO).astype(I32) + (position >= 2 * HALO).astype(I32) + (position >= 3 * HALO).astype(I32)
    partner_row = ints[:, 2 * SLOTS :] + group * HALO
    for k in range(3):
        at = slice(k * 128, k * 128 + 128)

        def put_rt(i, hit, at=at):
            rt[i * 128 : i * 128 + 128, at] = hit

        def put_r(i, hit, at=at):
            r[at, i * 128 : i * 128 + 128] = hit

        onehots(partner_row[:, at], 3, lane, sub, put_rt, put_r)
    row = lax.broadcasted_iota(I32, (1, D), 1)
    j = jnp.bitwise_xor(row >> 1, me[0])
    bit = [(j >> b) & 1 for b in range(8)]
    order = [
        bit[0], bit[1] ^ bit[2], bit[2], bit[6] ^ bit[7], bit[7], bit[3], bit[4] ^ bit[5], bit[5], row & 1,
    ]
    place = order[0]
    for b in order[1:]:
        place = 2 * place + b
    hits = jnp.broadcast_to(place, (D, D)) == lax.broadcasted_iota(I32, (D, D), 0)
    pick[...] = jnp.where(hits, 1.0, 0.0).astype(BF16)
    for at, rows, piece in ((0, E, m[...]), (E, HALO, core_in[HALO:, :]), (E + HALO, HALO, side_in[...])):
        w2[at : at + rows], w2[PAD + at : PAD + at + rows] = split(piece)
    w2[WIN:PAD] = jnp.zeros((PAD - WIN, D), BF16)
    w2[PAD + WIN :] = jnp.zeros((PAD - WIN, D), BF16)
    high, low = split(coeffs[...])
    c3[:16], c3[16:32], c3[32:] = high, high, low
    high, low = split(wb[...])
    w3[:16], w3[16:32], w3[32:] = high, low, high

    for i in range(SLOTS // CHUNK):
        at = slice(i * CHUNK, (i + 1) * CHUNK)
        weight = tn(c3[:, at], w3[...])
        rows = nn(ow[at, :], w2[...])
        tw[at, :] = weight
        gath[at, :] = rows
        th[at, :], tl[at, :] = split(rows * weight)
    agg[...] = nn(tt[...], th[...]) + nn(tt[...], tl[...])
    copy.wait()
    for l in range(2):
        wl_hi[l], wl_lo[l] = split(wl_s[l])


def slope(v, s):
    return s * (1.0 + v * (1.0 - s))


def middle(
    core_in, a1, a2, a3, m, cot, gath, tw, agg, t2, r, pick, coeffs, wr, wl_hi, wl_lo,
    out, gmp, gr_hi, gr_lo, wr_hi, wr_lo, wt_hi, wt_lo, own, send,
    g2, p, c_s, hs, gp_hi, gp_lo, left,
):
    scale = float(98304) ** -0.5
    arrived = jnp.concatenate([core_in[:HALO, :], a1[...], a2[...], a3[...]], axis=0)
    high, low = split(arrived)
    hs[2, :E] = nn(r[...], high).astype(BF16)
    hs[2, E:] = nn(r[...], low).astype(BF16)
    wr_hi[...], wr_lo[...] = split(wr[...])
    w_rev = (wr_hi[...], wr_lo[...])
    rp = dot3(nn, (hs[2, :E], hs[2, E:]), w_rev)
    left[2] = nt(pick[...], hs[2]).astype(BF16)
    rs = jax.nn.sigmoid(rp)
    gate = rp * rs
    h = m[...] + agg[...] + m[...] * gate
    pre, sig = [], []
    for l in range(2):
        hs[l, :E], hs[l, E:] = split(h)
        v = dot3(nn, (hs[l, :E], hs[l, E:]), (wl_hi[l], wl_lo[l]))
        left[l] = nt(pick[...], hs[l]).astype(BF16)
        s = jax.nn.sigmoid(v)
        pre.append(v)
        sig.append(s)
        h = h + v * s
    out[...] = h

    def weight_grad(k):
        gw = (nn(left[k], gp_hi[k]) + nn(left[k, :, :E], gp_lo[k])) * scale
        for half, ref in ((0, own), (256, send)):
            for part in range(4):
                first, last = max(part * PART, k * D), min(part * PART + PART, k * D + D)
                if first >= last:
                    continue
                if part == 0:
                    ref[:256, first:last] = gw[half : half + 256, first - k * D : last - k * D]
                    continue
                for block in range(16):
                    xa, xb, ya, yb = ((block >> b) & 1 for b in (3, 2, 1, 0))
                    to = ((xa, xb, ya, yb), (xb, xa, ya, yb), (ya, yb, xa, xb), (yb, ya, xa, xb))[part]
                    to = 16 * (8 * to[0] + 4 * to[1] + 2 * to[2] + to[3])
                    row = half + 16 * block
                    ref[to : to + 16, first:last] = gw[row : row + 16, first - k * D : last - k * D]

    g = cot[...]
    for l in (1, 0):
        high, low = split(g * slope(pre[l], sig[l]))
        gp_hi[l, :E], gp_hi[l, E:], gp_lo[l] = high, high, low
        g = g + dot3(nt, (gp_hi[l, :E], gp_lo[l]), (wl_hi[l], wl_lo[l]))
        weight_grad(l)
    g2[:E], g2[E:] = split(g)
    gmp[...] = g * (1.0 + gate)
    high, low = split(g * m[...] * slope(rp, rs))
    gp_hi[2, :E], gp_hi[2, E:], gp_lo[2] = high, high, low
    gr_hi[...], gr_lo[...] = high, low
    for i in range(SLOTS // CHUNK):
        at = slice(i * CHUNK, (i + 1) * CHUNK)
        prod = nn(t2[at, :], g2[...])
        p[0, at, :], p[1, at, :] = split(prod * gath[at, :])
        wt_hi[at, :], wt_lo[at, :] = split(prod * tw[at, :])
    weight_grad(2)
    c_s[:16], c_s[16:] = split(coeffs[...])
    both = nn(c_s[...], p[0])
    basis = (both[:16] + both[16:] + nn(c_s[:16], p[1])) * scale
    for ref in (own, send):
        ref[256:264, :512] = basis[:8]
        ref[256:264, 512:1024] = basis[8:]
        ref[256:264, 1024:] = jnp.zeros((8, 512), F32)


def scatter(ot, wt_hi, wt_lo, gmp, gr_hi, gr_lo, rt, wr_hi, wr_lo, gm, core_out, side_out, gr1, gr2, gr3):
    q = (nn(rt[...], gr_hi[...]).astype(BF16), nn(rt[...], gr_lo[...]).astype(BF16))
    rims = nn(ot[E:, :], wt_hi[...]) + nn(ot[E:, :], wt_lo[...])
    rows = dot3(nt, q, (wr_hi[...], wr_lo[...]))
    core_out[:HALO] = rows[:HALO]
    core_out[HALO:] = rims[:HALO]
    side_out[...] = rims[HALO:]
    for k, ref in enumerate((gr1, gr2, gr3)):
        ref[...] = rows[(k + 1) * HALO : (k + 2) * HALO]
    gm[...] = gmp[...] + (nn(ot[:E, :], wt_hi[...]) + nn(ot[:E, :], wt_lo[...]))


def finish(me, gm, core_in, g1, g2, g3, side_in, out):
    odd = me[0] & 1
    out[:HALO] = gm[:HALO] + core_in[:HALO]
    for k, ref in enumerate((g1, g2, g3)):
        at = slice((k + 1) * HALO, (k + 2) * HALO)
        out[at] = gm[at] + ref[...]
    last = E - HALO
    at = pl.ds(pl.multiple_of(last * (1 - odd), 32), HALO)
    out[at, :] = out[at, :] + core_in[HALO:]
    at = pl.ds(pl.multiple_of(last * odd, 32), HALO)
    out[at, :] = out[at, :] + side_in[...]


def halves(rows, extra, keep, send):
    n = rows.shape[0] // 2
    keep[...] = rows[:n]
    send[:n] = rows[n:]
    send[n:] = extra


def fold_core(own, got, *refs):
    for part in range(4):
        at = slice(part * PART, (part + 1) * PART)
        halves(own[:256, at] + got[:256, at], own[256:, at] + got[256:, at], refs[2 * part], refs[2 * part + 1])


def fold_merge(keep_1, send_1, got_1, keep_2, send_2, got_2, keep_next, send_next):
    n = keep_1.shape[0]
    for at, keep, send, got in ((slice(0, PART), keep_1, send_1, got_1), (slice(PART, HALF), keep_2, send_2, got_2)):
        rows = keep[...] + got[:n]
        keep_next[:, at] = rows[: n // 2]
        send_next[: n // 2, at] = rows[n // 2 :]
        send_next[n // 2 :, at] = send[n:] + got[n:]


def fold(keep, send, got, keep_next, send_next):
    n = keep.shape[0]
    halves(keep[...] + got[:n], send[n:] + got[n:], keep_next, send_next)


BASIS = 2 * D


def fold_join(keep_a, send_a, got_a, keep_b, send_b, got_b, keep_next, send_next):
    n = keep_a.shape[0]
    for at, keep, send, got in ((0, keep_a, send_a, got_a), (HALF, keep_b, send_b, got_b)):
        rows = keep[...] + got[:n]
        extra = send[n:] + got[n:]
        width = min(HALF, BASIS - at)
        keep_next[:, at : at + HALF] = rows[:8]
        send_next[:, at : at + width] = extra[:, :width]
        send_next[:, BASIS + at : BASIS + at + HALF] = rows[8:]


def fold_z0(keep, send, got, keep_next, send_next):
    rows = keep[...] + got[:, BASIS:]
    keep_next[...] = rows[:4]
    send_next[:, :BASIS] = send[:, :BASIS] + got[:, :BASIS]
    send_next[:4, BASIS:] = rows[4:, :HALF]
    send_next[4:, BASIS:] = rows[4:, HALF:]


def fold_z1(keep, send, got, keep_next, send_next):
    send_next[:, :BASIS] = send[:, :BASIS] + got[:, :BASIS]
    for k in range(2):
        rows = keep[:, k * HALF : k * HALF + HALF] + got[4 * k : 4 * k + 4, BASIS:]
        keep_next[:, k * HALF : k * HALF + HALF] = rows[:2]
        for i in range(2):
            q = 2 * k + i
            send_next[2 * q : 2 * q + 2, BASIS:] = rows[2:, i * PART : i * PART + PART]


def fold_last(keep, send, got, layers, rev, basis):
    extra = send[:, :BASIS] + got[:, :BASIS]
    basis[:8] = extra[:, :D]
    basis[8:] = extra[:, D:]
    for q in range(4):
        rows = keep[:, q * PART : q * PART + PART] + got[2 * q : 2 * q + 2, BASIS:]
        for k in range(3):
            first, last = max(q * PART, k * D), min(q * PART + PART, k * D + D)
            for a in range(2):
                if first < last:
                    piece = rows[a : a + 1, first - q * PART : last - q * PART]
                    at = a * D + first - k * D
                    if k < 2:
                        layers[k : k + 1, at : at + last - first] = piece
                    else:
                        rev[:, at : at + last - first] = piece


def call(kernel, outs, specs, scratch=(), flops=1_000_000, grant=8):
    places = {
        "s": pl.BlockSpec(memory_space=pltpu.SMEM),
        "v": pl.BlockSpec(memory_space=pltpu.VMEM),
        "h": pl.BlockSpec(memory_space=pltpu.HBM),
    }
    return pl.pallas_call(
        kernel,
        out_shape=[jax.ShapeDtypeStruct(shape, dtype) for shape, dtype in outs],
        in_specs=[places[c] for c in specs],
        out_specs=[places["v"]] * len(outs),
        scratch_shapes=list(scratch),
        compiler_params=pltpu.CompilerParams(vmem_limit_bytes=grant << 20),
        cost_estimate=pl.CostEstimate(flops=flops, bytes_accessed=1 << 20, transcendentals=0),
    )


def swap(value, mask):
    count = lax.axis_size("edges")
    return lax.ppermute(value, "edges", [(i, i ^ mask) for i in range(count)])


def swap_side(value):
    count = lax.axis_size("edges")
    return lax.ppermute(value, "edges", [(i, (i + (1 if i % 2 else -1)) % count) for i in range(count)])


def tie(value, *others):
    return lax.optimization_barrier((value, *others))[0]


def step(state, got):
    keep, send = state
    n, columns = keep.shape
    return call(fold, [((n // 2, columns), F32), ((n // 2 + 8, columns), F32)], "vvv")(keep, send, got)


def on_device_body(messages, rev_slot, tri_basis, tri_source, tri_target, tile_block, tile_count, w_basis, w_rev, w_layers, cotangent):
    index = lax.axis_index("edges").astype(I32)
    me = index.reshape(1)
    odd = index & 1
    quarter = ((HALO, D), F32)
    toward_core = lax.dynamic_slice_in_dim(messages, (E - HALO) * (1 - odd), HALO)
    toward_side = lax.dynamic_slice_in_dim(messages, (E - HALO) * odd, HALO)
    a2 = swap(messages[2 * HALO : 3 * HALO], 32)
    side_in = swap_side(toward_side)
    core_in = swap(jnp.concatenate([messages[:HALO], toward_core], axis=0), 1)
    a3 = swap(messages[3 * HALO :], 128)
    a1 = swap(messages[HALO : 2 * HALO], 4)
    (gath, tw, agg, ot, t2, r, rt, pick, wl_hi, wl_lo) = call(
        prepare,
        [
            ((SLOTS, D), F32), ((SLOTS, D), F32), ((E, D), F32), ((WIN, SLOTS), BF16), ((SLOTS, 2 * E), BF16),
            ((E, E), BF16), ((E, E), BF16), ((D, D), BF16),
            ((2, D, D), BF16), ((2, D, D), BF16),
        ],
        "sss" + "v" * 8 + "h",
        [
            pltpu.VMEM((1, 2 * SLOTS + E), I32),
            pltpu.VMEM((SLOTS, 2 * PAD), BF16), pltpu.VMEM((2 * PAD, D), BF16), pltpu.VMEM((E, SLOTS), BF16),
            pltpu.VMEM((SLOTS, D), BF16), pltpu.VMEM((SLOTS, D), BF16),
            pltpu.VMEM((48, SLOTS), BF16), pltpu.VMEM((48, D), BF16),
            pltpu.VMEM((2, D, D), F32), pltpu.SemaphoreType.DMA,
        ],
        flops=4_000_000_000,
        grant=26,
    )(me, tile_count, tile_block, tri_source, tri_target, rev_slot, tri_basis, w_basis, messages, core_in, side_in, w_layers)
    out, gmp, gr_hi, gr_lo, wr_hi, wr_lo, wt_hi, wt_lo, own, send = call(
        middle,
        [
            ((E, D), F32), ((E, D), F32), ((E, D), BF16), ((E, D), BF16), ((D, D), BF16), ((D, D), BF16),
            ((SLOTS, D), BF16), ((SLOTS, D), BF16), ((264, 3 * D), F32), ((264, 3 * D), F32),
        ],
        "v" * 16,
        [
            pltpu.VMEM((2 * E, D), BF16), pltpu.VMEM((2, SLOTS, D), BF16), pltpu.VMEM((32, SLOTS), BF16),
            pltpu.VMEM((3, 2 * E, D), BF16), pltpu.VMEM((3, 2 * E, D), BF16), pltpu.VMEM((3, E, D), BF16),
            pltpu.VMEM((3, D, 2 * E), BF16),
        ],
        flops=16_000_000_000,
        grant=16,
    )(core_in, a1, a2, a3, messages, cotangent, gath, tw, agg, t2, r, pick, tri_basis, w_rev, wl_hi, wl_lo)

    got = swap(send, 1)
    gm, core_out, side_out, gr1, gr2, gr3 = call(
        scatter,
        [((E, D), F32), ((2 * HALO, D), F32)] + [quarter] * 4,
        "v" * 9,
        flops=1_000_000_000,
        grant=8,
    )(ot, wt_hi, wt_lo, gmp, gr_hi, gr_lo, rt, wr_hi, wr_lo)
    b2 = swap(gr2, 32)
    core_back = swap(core_out, 1)
    side_back = swap_side(side_out)
    b1 = swap(gr1, 4)
    b3 = swap(gr3, 128)
    (grad_messages,) = call(finish, [((E, D), F32)], "s" + "v" * 6)(me, gm, core_back, b1, b2, b3, side_back)
    parts = call(fold_core, [((128, PART), F32), ((136, PART), F32)] * 4, "vv")(own, got)
    parts = [parts[2 * k : 2 * k + 2] for k in range(4)]
    gots = [swap(part[1], mask) for part, mask in zip(parts, (2, 6, 64, 192))]
    parts = [step(part, arrived) for part, arrived in zip(parts, gots)]
    gots = [swap(part[1], mask) for part, mask in zip(parts, (6, 2, 192, 64))]
    a, b = (
        call(fold_merge, [((32, HALF), F32), ((40, HALF), F32)], "v" * 6)(
            *parts[k], gots[k], *parts[k + 1], gots[k + 1]
        )
        for k in (0, 2)
    )
    got_a, got_b = swap(a[1], 64), swap(b[1], 2)
    a, b = step(a, got_a), step(b, got_b)
    got_a, got_b = swap(a[1], 192), swap(b[1], 6)
    c = call(fold_join, [((8, 3 * D), F32), ((8, BASIS + 3 * D), F32)], "v" * 6)(*a, got_a, *b, got_b)
    c = call(fold_z0, [((4, 3 * D), F32), ((8, BASIS + HALF), F32)], "vvv")(*c, swap(c[1], 8))
    c = call(fold_z1, [((2, 3 * D), F32), ((8, BASIS + PART), F32)], "vvv")(*c, swap(c[1], 16))
    got = tie(swap(c[1], 48), grad_messages)
    layers, rev, basis = call(fold_last, [((2, 2 * D), F32), ((1, 2 * D), F32), ((16, D), F32)], "vvv")(*c, got)
    return (out, grad_messages, layers, rev.reshape(2 * D), basis)


def solution(mesh):
    split_rows, flat = P("edges", None), P("edges")
    in_specs = (split_rows, flat, P(None, "edges"), flat, flat, flat, flat, P(), P(), P(), split_rows)
    out_specs = (split_rows, split_rows, P(None, "edges"), flat, P())
    return jax.shard_map(on_device_body, mesh=mesh, in_specs=in_specs, out_specs=out_specs, check_vma=False)
```
